128 devices in a mesh: lon: 16 (over z, x_hi, core), lat: 8 (over x_lo, y).
Axes of the slice: x: 4 (x_hi: 2, x_lo: 2; x = x_hi * 2 + x_lo), y: 4, z: 4, core: 2. Of those that a mesh axis runs over, the one named last changes fastest.
Arguments:
- innovations: bfloat16 [7, 16384, 16, 128], P(None, ('lon', 'lat')), may hold values from -6 to 6
- fractions: bfloat16 [7, 16384, 2, 128], P(None, ('lon', 'lat')), may hold values from 0 to 1
- cell_index: int32 [7, 16384, 128], P(None, ('lon', 'lat')), may hold values from 0 to 238, as said below
- counts: int32 [7, 16384, 2], P(None, ('lon', 'lat')), may hold values from 0 to 64, as said below
- blocks: int32 [7, 16384, 2], P(None, ('lon', 'lat')), may hold values from 0 to 15
- u_wind: float32 [4, 256, 2048], P(None, 'lat', 'lon'), may hold values from -0.5 to 0.5
- v_wind: float32 [4, 256, 2048], P(None, 'lat', 'lon'), may hold values from -0.5 to 0.5
- channel_mix: float32 [16, 16], replicated
Outputs:
- gradient: float32 [4, 4, 256, 2048], P(None, None, 'lat', 'lon')
The draws below stay inside these ranges and needn't reach their ends.
Inputs may be any that keep to these rules, and one draw needn't show every extreme that they name: Row and column of a cell inside its tile, cell_index // 16 and cell_index % 16, are each at most 14. `counts`: in every draw some receiving device gets 64 live observations in every tile from every sender.
All inputs are finite; a program needn't handle non-finite values.
Results may differ from the reference program's by a relative error of at most 0.0003.
Values may be sent and summed in bfloat16 or wider, within the bound.
No kernel may reach another device: no remote copies, remote signals or barrier semaphores. Data moves between devices by JAX's collectives and lax.ppermute only.
A program may use at most 192 MiB of HBM per device.

```python
import math
import jax
import jax.numpy as jnp
from jax import lax

VARS = 4
LEV = 4
CH = 16
TILE = 16
J = 64
CAP = 2
SLOTS = 7
CLAT = 32
CLON = 128
NLAT = 256
NLON = 2048
BLOCKS_DEV = 16
N_LAT = 8
DEVICES = 128


def draw_cell_index(key, part):
    first, second, third = jax.random.split(key, 3)
    shape = (SLOTS, DEVICES * DEVICES, CAP * J)
    row_part = jax.random.randint(first, shape, 0, TILE - 1)
    col_part = jax.random.randint(second, shape, 0, TILE - 1)
    cell_all = (row_part * TILE + col_part).reshape(-1)
    where_top = jax.random.randint(third, (), 0, cell_all.shape[0])
    cell_all = cell_all.at[where_top].set(TILE * TILE - TILE - 2)
    return cell_all.reshape(shape).astype(jnp.int32)


def draw_counts(key, part):
    first, second, third = jax.random.split(key, 3)
    shape = (SLOTS, DEVICES * DEVICES, CAP)
    base_count = jax.random.randint(first, shape, 0, J + 1)
    dense_dest = jax.random.randint(second, (DEVICES,), 0, 4) == 0
    chosen = jax.random.randint(third, (), 0, DEVICES)
    dense_dest = dense_dest.at[chosen].set(True)
    dense_pair = jnp.tile(dense_dest, DEVICES)[None, :, None]
    return jnp.where(dense_pair, J, base_count // 2).astype(jnp.int32)


def draw_channel_mix(key, part):
    first, second = jax.random.split(key, 2)
    diagonal = jax.random.uniform(first, (CH,), jnp.float32, 0.5, 1.0)
    off_part = 0.25 / math.sqrt(CH) * jax.random.normal(second, (CH, CH), jnp.float32)
    return (off_part + jnp.eye(CH, dtype=jnp.float32) * diagonal[None, :]).astype(jnp.float32)


def with_ends(values, key, smallest, high):
    shape = values.shape
    spot = [jax.random.randint(jax.random.fold_in(key, axis), (), 0, shape[axis]) for axis in range(len(shape))]
    values = values.at[tuple(spot)].set(smallest)
    longest = shape.index(max(shape))
    spot[longest] = (spot[longest] + 1) % shape[longest]
    return values.at[tuple(spot)].set(high)


def level_of(own_key, dims, pieces, low, high):
    def one(position, shards_of):
        steps = jax.random.uniform(jax.random.fold_in(jax.random.fold_in(own_key, 6), position), (shards_of,), jnp.float32, low / len(pieces), high / len(pieces))
        return jnp.repeat(jnp.exp(steps), dims[position] // shards_of).reshape((-1,) + (1,) * (len(dims) - position - 1))

    loudness = one(*pieces[0])
    for cut in pieces[1:]:
        loudness = loudness * one(*cut)
    return loudness


def scatter_about(rng, dims, scale, most, cuts=(), kind=jnp.bfloat16):
    result = jax.random.normal(rng, dims, jnp.float32) * scale
    if len(cuts) > 0:
        result = level_of(rng, dims, cuts, -0.22, 0.18) * result
    return jnp.clip(result, min=-most, max=most).astype(kind)


def setup_inputs(seed: int = 0) -> dict:
    keys = jax.random.split(jax.random.key(seed), 9)
    return {
        "innovations": scatter_about(keys[0], (SLOTS, DEVICES * DEVICES, CH, CAP * J), 1.0, 6.0, ((1, 128),)),
        "fractions": jnp.clip(1.0 * jax.random.uniform(keys[1], (SLOTS, DEVICES * DEVICES, 2, CAP * J), jnp.float32) ** level_of(keys[1], (SLOTS, DEVICES * DEVICES, 2, CAP * J), ((1, 128),), -0.2, 0.2), 0.0, 1.0).astype(jnp.bfloat16),
        "cell_index": draw_cell_index(jax.random.fold_in(keys[8], 71), 0),
        "counts": draw_counts(jax.random.fold_in(keys[8], 71), 0),
        "blocks": with_ends(jax.random.randint(keys[4], (SLOTS, DEVICES * DEVICES, CAP), 0, BLOCKS_DEV), jax.random.fold_in(keys[4], 1), 0, BLOCKS_DEV - 1).astype(jnp.int32),
        "u_wind": jnp.clip(jax.random.uniform(keys[5], (LEV, NLAT, NLON), jnp.float32, -0.5, 0.5) * level_of(keys[5], (LEV, NLAT, NLON), ((1, 8), (2, 16)), -0.4, 0.0), -0.5, 0.5),
        "v_wind": jnp.clip(jax.random.uniform(keys[6], (LEV, NLAT, NLON), jnp.float32, -0.5, 0.5) * level_of(keys[6], (LEV, NLAT, NLON), ((1, 8), (2, 16)), -0.4, 0.0), -0.5, 0.5),
        "channel_mix": draw_channel_mix(jax.random.fold_in(keys[8], 71), 0),
    }


KAPPA = 0.125
HIGHEST = lax.Precision.HIGHEST


def lat_next(layer_stack):
    return jnp.pad(layer_stack, ((0, 0), (0, 0), (0, 1), (0, 0)))[:, :, 1:, :]


def lat_prev(layer_stack):
    return jnp.pad(layer_stack, ((0, 0), (0, 0), (1, 0), (0, 0)))[:, :, :-1, :]


def adjoint_op(adjoint_field, u_wind, v_wind, channel_mix):
    mixed = jnp.einsum('dc,dn->cn', channel_mix, adjoint_field.reshape(CH, NLAT * NLON), precision=HIGHEST)
    mixed = mixed.reshape(VARS, LEV, NLAT, NLON)
    east_flux = u_wind[None] * mixed
    north_flux = v_wind[None] * mixed
    spread = jnp.roll(mixed, -1, 3) + jnp.roll(mixed, 1, 3) + lat_next(mixed) + lat_prev(mixed)
    carry_term = 0.5 * (jnp.roll(east_flux, -1, 3) - jnp.roll(east_flux, 1, 3)) + 0.5 * (lat_next(north_flux) - lat_prev(north_flux))
    return (1.0 - 4.0 * KAPPA) * mixed + KAPPA * spread + carry_term


def slot_forcing(innov_slot, frac_slot, cell_slot, count_slot, block_slot):
    pairs = DEVICES * DEVICES
    width = CAP * J
    slot_pos = jnp.arange(width, dtype=jnp.int32)
    tile_of = slot_pos // J
    count_each = count_slot[:, tile_of]
    is_live = (slot_pos % J)[None, :] < count_each
    block_each = block_slot[:, tile_of]
    target = jnp.arange(pairs, dtype=jnp.int32) % DEVICES
    lon_index = target // N_LAT
    lat_index = target % N_LAT
    across = CLON // TILE
    row_base = (lat_index * CLAT)[:, None] + (block_each // across) * TILE + cell_slot // TILE
    col_base = (lon_index * CLON)[:, None] + (block_each % across) * TILE + cell_slot % TILE
    frac_y = frac_slot[:, 0, :].astype(jnp.float32)
    frac_x = frac_slot[:, 1, :].astype(jnp.float32)
    live_mask = jnp.where(is_live, 1.0, 0.0).astype(jnp.float32)
    values = jnp.transpose(innov_slot.astype(jnp.float32), (0, 2, 1))
    grid_sum = jnp.zeros((NLAT * NLON, CH), jnp.float32)
    corners = ((0, 0, (1.0 - frac_y) * (1.0 - frac_x)), (0, 1, (1.0 - frac_y) * frac_x),
               (1, 0, frac_y * (1.0 - frac_x)), (1, 1, frac_y * frac_x))
    for shift_y, shift_x, weight in corners:
        flat_index = ((row_base + shift_y) * NLON + col_base + shift_x).reshape(-1).astype(jnp.int32)
        update = (values * (weight * live_mask)[:, :, None]).reshape(-1, CH)
        grid_sum = grid_sum.at[flat_index].add(update)
    return jnp.transpose(grid_sum.reshape(NLAT, NLON, VARS, LEV), (2, 3, 0, 1))


def reference(innovations, fractions, cell_index, counts, blocks, u_wind, v_wind, channel_mix):
    forcing = [slot_forcing(innovations[slot], fractions[slot], cell_index[slot], counts[slot], blocks[slot])
               for slot in range(SLOTS)]
    adjoint_field = forcing[SLOTS - 1]
    for later in range(SLOTS - 2, -1, -1):
        adjoint_field = adjoint_op(adjoint_field, u_wind, v_wind, channel_mix) + forcing[later]
    return adjoint_field
```

```python
import functools

import jax
import jax.numpy as jnp
from jax import lax
from jax.experimental import pallas as pl
from jax.experimental.pallas import tpu as pltpu
from jax.sharding import PartitionSpec as P

VARS = 4
LEV = 4
CH = 16
TILE = 16
LANES = 128
KAPPA = 0.125
AXES = ("lon", "lat")
F32 = jnp.float32
BF16 = jnp.bfloat16


def offsets_of(widths):
    starts, total = [], 0
    for width in widths:
        starts.append(total)
        total += width
    return starts, total


def pack_rows(slots):
    used = slots * (CH + 3) + 1
    return used, -(-used // 8) * 8


def build_payload(innovations, fractions, cell_index, counts, blocks):
    slots, targets, channels, width = innovations.shape
    tiles = counts.shape[2]
    per_tile = width // tiles
    lane = lax.broadcasted_iota(jnp.int32, (1, 1, width), 2)
    first = lane < per_tile
    count_lane = jnp.where(first, counts[:, :, 0:1], counts[:, :, 1:2])
    block_lane = jnp.where(first, blocks[:, :, 0:1], blocks[:, :, 1:2])
    is_live = (lane & (per_tile - 1)) < count_lane
    values = jnp.where(is_live[:, :, None, :], innovations, jnp.zeros((), BF16))
    row = cell_index >> 4
    column = cell_index & 15
    skewed = (row >> 3) * LANES + ((row + block_lane) & 7) * TILE + column
    used, rows = pack_rows(slots)
    spots = jnp.transpose(blocks, (1, 0, 2)).reshape(targets, 1, slots * tiles)
    spots = jnp.pad(spots, ((0, 0), (0, rows - used), (0, LANES - slots * tiles)))
    return jnp.concatenate(
        [
            jnp.transpose(values, (1, 0, 2, 3)).reshape(targets, slots * channels, width),
            jnp.transpose(fractions, (1, 0, 2, 3)).reshape(targets, slots * 2, width),
            jnp.transpose(skewed, (1, 0, 2)).astype(BF16),
            spots.astype(BF16),
        ],
        axis=1,
    )


def scatter_kernel(slots, batch, widths, blocks_ref, got_ref, out_ref, *rest):
    if widths:
        top_ref, bottom_ref, acc_ref, place_ref, below_ref = rest
    else:
        acc_ref, place_ref, below_ref = rest
    step = pl.program_id(0)
    rows_out = out_ref.shape[1]

    @pl.when(step == 0)
    def _():
        acc_ref[...] = jnp.zeros_like(acc_ref)
        place_ref[...] = lax.broadcasted_iota(jnp.int32, place_ref.shape, 0).astype(F32).astype(BF16)

    first = lax.broadcasted_iota(jnp.int32, (1, LANES), 1) < LANES // 2
    first_mask = jnp.where(first, 1.0, 0.0).astype(BF16)
    second_mask = jnp.where(first, 0.0, 1.0).astype(BF16)
    base = slots * CH

    def one(index, carry):
        sender = step * batch + index
        aux = got_ref[index, pl.ds(base, 3 * slots), :].astype(F32)
        for slot in range(slots):
            value = got_ref[index, pl.ds(slot * CH, CH), :].astype(F32)
            frac_y = aux[2 * slot : 2 * slot + 1, :]
            frac_x = aux[2 * slot + 1 : 2 * slot + 2, :]
            cell = aux[2 * slots + slot : 2 * slots + slot + 1, :].astype(BF16)
            by_x = value * frac_x
            by_y = value * frac_y
            both = jnp.concatenate([value, by_x, by_y, by_x * frac_y], axis=0)
            high = both.astype(BF16)
            low = (both - high.astype(F32)).astype(BF16)
            wide = jnp.concatenate([high, low], axis=1)
            mask_a = jnp.concatenate([first_mask, first_mask], axis=1)
            mask_b = jnp.concatenate([second_mask, second_mask], axis=1)
            left = jnp.concatenate([wide * mask_a, wide * mask_b], axis=0)
            onehot = jnp.where(place_ref[...] == cell, jnp.ones((), BF16), jnp.zeros((), BF16))
            right = jnp.concatenate([onehot, onehot], axis=1)
            sums = lax.dot_general(left, right, (((1,), (1,)), ((), ())), preferred_element_type=F32)
            spot = (sender * slots + slot) * 2
            acc_ref[slot, blocks_ref[spot]] += sums[: 4 * CH]
            acc_ref[slot, blocks_ref[spot + 1]] += sums[4 * CH :]
        return carry

    lax.fori_loop(0, batch, one, 0)

    @pl.when(step == pl.num_programs(0) - 1)
    def _():
        group = lax.broadcasted_iota(jnp.int32, (CH, LANES), 1) >> 4

        def part(number, carry):
            slot = number >> 2
            band = (number >> 1) & 1
            half = number & 1
            straight = [jnp.zeros((CH, LANES), F32)] * 8
            under = [jnp.zeros((CH, LANES), F32)] * 8
            for column in range(8):
                tile = acc_ref[slot, band * 8 + column, :, pl.ds(pl.multiple_of(half * LANES, LANES), LANES)]
                a_0, a_x = tile[:CH], tile[CH : 2 * CH]
                a_y, a_xy = tile[2 * CH : 3 * CH], tile[3 * CH :]
                here = a_0 - a_x - a_y + a_xy + pltpu.roll(a_x - a_xy, 1, 1)
                next_row = a_y - a_xy + pltpu.roll(a_xy, 1, 1)
                for y in range(8):
                    hit = group == ((y + column) & 7)
                    straight[y] = jnp.where(hit, here, straight[y])
                    under[y] = jnp.where(hit, next_row, under[y])
            for y in range(8):
                turn = (-16 * y) % LANES
                row = band * 16 + half * 8 + y
                out_ref[slot, row] = pltpu.roll(straight[y], turn, 1) if turn else straight[y]
                below_ref[slot, row] = pltpu.roll(under[y], turn, 1) if turn else under[y]
            return carry

        lax.fori_loop(0, 4 * slots, part, 0)

        def shift(slot, carry):
            out_ref[slot, 1:] += below_ref[slot, : rows_out - 1]
            return carry

        lax.fori_loop(0, slots, shift, 0)
        if widths:
            starts, _ = offsets_of(widths)
            for slot, (start, width) in enumerate(zip(starts, widths)):
                top_ref[start : start + width] = out_ref[slot, :width]
                bottom_ref[start : start + width] = out_ref[slot, rows_out - width :]


def scatter(got, slots, widths, rows_out):
    senders, rows, _ = got.shape
    base = slots * (CH + 3)
    blocks = got[:, base, : 2 * slots].astype(jnp.int32).reshape(-1)
    batch = 8
    _, total = offsets_of(widths)
    whole = lambda shape: pl.BlockSpec(shape, lambda i, b: (0,) * len(shape))
    shapes = [(slots, rows_out, CH, LANES)] + ([(total, CH, LANES)] * 2 if widths else [])
    return pl.pallas_call(
        functools.partial(scatter_kernel, slots, batch, widths),
        grid_spec=pltpu.PrefetchScalarGridSpec(
            num_scalar_prefetch=1,
            grid=(senders // batch,),
            in_specs=[pl.BlockSpec((batch, rows, LANES), lambda i, b: (i, 0, 0))],
            out_specs=[whole(s) for s in shapes],
            scratch_shapes=[
                pltpu.VMEM((slots, 16, 4 * CH, 2 * LANES), F32),
                pltpu.VMEM((2 * LANES, LANES), BF16),
                pltpu.VMEM((slots, rows_out, CH, LANES), F32),
            ],
        ),
        out_shape=[jax.ShapeDtypeStruct(s, F32) for s in shapes],
        name="scatter",
    )(blocks, got)


GROUPS = 4
SPAN = LANES // GROUPS


def lane_pack_kernel(widths, halo, forcing_ref, above_ref, below_ref, left_ref, right_ref, tall_ref):
    rows_own = forcing_ref.shape[1]
    per_group = left_ref.shape[0]
    starts, _ = offsets_of(widths)
    tall_ref[...] = jnp.zeros_like(tall_ref)
    for slot, (start, width) in enumerate(zip(starts, widths)):
        tall_ref[slot, halo - width : halo] = above_ref[start : start + width]
        tall_ref[slot, halo : halo + rows_own] = forcing_ref[slot]
        tall_ref[slot, halo + rows_own : halo + rows_own + width] = below_ref[start : start + width]
    lane = lax.broadcasted_iota(jnp.int32, (CH, LANES), 1)

    def one(row, carry):
        to_left = jnp.zeros((CH, LANES), F32)
        to_right = jnp.zeros((CH, LANES), F32)
        for group in range(GROUPS):
            for slot, (start, width) in enumerate(zip(starts, widths)):
                source = tall_ref[slot, group * per_group + row]
                begin = group * SPAN + start
                hit = (lane >= begin) & (lane < begin + width)
                to_left = jnp.where(hit, pltpu.roll(source, begin, 1) if begin else source, to_left)
                to_right = jnp.where(hit, pltpu.roll(source, (begin + width) % LANES, 1), to_right)
        left_ref[row] = to_left
        right_ref[row] = to_right
        return carry

    lax.fori_loop(0, per_group, one, 0)


def lane_pack(forcing, above, below, widths, halo):
    tall = forcing.shape[1] + 2 * halo
    shape = jax.ShapeDtypeStruct((tall // GROUPS, CH, LANES), F32)
    slots = len(widths)
    return pl.pallas_call(
        functools.partial(lane_pack_kernel, widths, halo),
        grid=(1,),
        in_specs=[
            pl.BlockSpec((slots,) + forcing.shape[1:], lambda i: (0, 0, 0, 0)),
            pl.BlockSpec(above.shape, lambda i: (0, 0, 0)),
            pl.BlockSpec(below.shape, lambda i: (0, 0, 0)),
        ],
        out_specs=[pl.BlockSpec(shape.shape, lambda i: (0, 0, 0))] * 2,
        out_shape=[shape, shape],
        scratch_shapes=[pltpu.VMEM((slots, tall, CH, LANES), F32)],
        name="lane_pack",
    )(forcing, above, below)


def march_kernel(
    widths, halo, edge_ref, forcing_ref, above_ref, below_ref, west_ref, east_ref, u_ref, v_ref, mix_ref, out_ref,
    field_ref, extra_ref, turn_ref,
):
    rows_own = forcing_ref.shape[1]
    tall = rows_own + 2 * halo
    per_group = west_ref.shape[0]
    starts, _ = offsets_of(widths)
    lane = lax.broadcasted_iota(jnp.int32, (CH, LANES), 1)
    main = pl.ds(0, LANES)
    side = pl.ds(LANES, LANES)

    for slot, (start, width) in enumerate(zip(starts, widths)):
        lo, hi = halo - width, halo + rows_own + width
        extra_ref[slot, lo:halo, :, main] = above_ref[start : start + width]
        extra_ref[slot, halo : halo + rows_own, :, main] = forcing_ref[slot]
        extra_ref[slot, halo + rows_own : hi, :, main] = below_ref[start : start + width]

    def edges(row, carry):
        west = west_ref[row]
        east = east_ref[row]
        for group in range(GROUPS):
            for slot, (start, width) in enumerate(zip(starts, widths)):
                begin = group * SPAN + start
                east_turn = (-begin) % LANES
                value = jnp.where(lane < width, pltpu.roll(east, east_turn, 1) if east_turn else east, 0.0)
                west_turn = (LANES - width - begin) % LANES
                value = jnp.where(
                    lane >= LANES - width, pltpu.roll(west, west_turn, 1) if west_turn else west, value
                )
                extra_ref[slot, group * per_group + row, :, side] = value
        return carry

    lax.fori_loop(0, per_group, edges, 0)

    first_row = jnp.where(edge_ref[0] == 1, halo, 0)
    last_row = jnp.where(edge_ref[1] == 1, halo + rows_own, tall)
    turns = [jnp.broadcast_to(mix_ref[:, d : d + 1], (CH, LANES)) for d in range(CH)]
    turn_ref[0] = jnp.zeros((CH, LANES), F32)

    slots = len(widths)
    for number in range(slots):
        reach = widths[number]
        source = extra_ref.at[0] if number == 0 else field_ref.at[number % 2]
        target = field_ref.at[(number + 1) % 2]
        begin, end = halo - reach, halo + rows_own + reach
        last = number == slots - 1
        tiles = 1 if last else 2

        def one(row, carry, source=source, target=target, last=last, number=number):
            done_before, flux_two, flux_one = carry
            inside = (row >= first_row) & (row < last_row)
            mixed = []
            for tile in (main, side):
                total = jnp.zeros((CH, LANES), F32)
                for d in range(CH):
                    total = total + turns[d] * jnp.broadcast_to(source[row, d : d + 1, tile], (CH, LANES))
                mixed.append(jnp.where(inside, total, 0.0))
            mixed = jnp.concatenate(mixed, axis=1)
            u_half = jnp.concatenate([u_ref[row]] * 2, axis=0) * 0.5
            v_half = jnp.concatenate([v_ref[row]] * 2, axis=0) * 0.5
            own = (1.0 - 4.0 * KAPPA) * mixed
            own = own + pltpu.roll((KAPPA + u_half) * mixed, 2 * LANES - 1, 1)
            own = own + pltpu.roll((KAPPA - u_half) * mixed, 1, 1)
            up = (KAPPA + v_half) * mixed
            down = (KAPPA - v_half) * mixed
            result = done_before + up + flux_two
            before = jnp.maximum(row - 1, 0)
            if last:
                turn_ref[jnp.clip(row - 1 - halo, 0, rows_own - 1)] = (
                    result[:, :LANES] + forcing_ref[slots, jnp.clip(row - 1 - halo, 0, rows_own - 1)]
                )
            else:
                target[before] = result + extra_ref[number + 1, before]
            return own, flux_one, down

        zero = jnp.concatenate([turn_ref[0], turn_ref[0]], axis=1)
        lax.fori_loop(begin, end, one, (zero, zero, zero))

    for channel in range(CH):
        out_ref[channel] = turn_ref[:, channel, :]


def march(edge, forcing, above, below, west, east, u_tall, v_tall, mix, widths, halo):
    rows_own = forcing.shape[1]
    tall = rows_own + 2 * halo
    slots = len(widths)
    vmem = pl.BlockSpec(memory_space=pltpu.VMEM)
    return pl.pallas_call(
        functools.partial(march_kernel, widths, halo),
        in_specs=[pl.BlockSpec(memory_space=pltpu.SMEM)] + [vmem] * 8,
        out_specs=vmem,
        out_shape=jax.ShapeDtypeStruct((CH, rows_own, LANES), F32),
        scratch_shapes=[
            pltpu.VMEM((2, tall, CH, 2 * LANES), F32),
            pltpu.VMEM((slots, tall, CH, 2 * LANES), F32),
            pltpu.VMEM((rows_own, CH, LANES), F32),
        ],
        name="march",
    )(edge, forcing, above, below, west, east, u_tall, v_tall, mix)


def ring(axis, wrap):
    count = lax.axis_size(axis)
    up = [(i, (i + 1) % count) for i in range(count if wrap else count - 1)]
    return up, [(j, i) for i, j in up]


def wind_tables(u_wind, v_wind, halo):
    both = jnp.stack([u_wind, v_wind])
    for axis, dim, wrap in (("lat", 2, False), ("lon", 3, True)):
        up, down = ring(axis, wrap)
        length = both.shape[dim]
        before = lax.ppermute(lax.slice_in_dim(both, length - halo, length, axis=dim), axis, up)
        after = lax.ppermute(lax.slice_in_dim(both, 0, halo, axis=dim), axis, down)
        if dim == 2:
            both = jnp.concatenate([before, both, after], axis=dim)
        else:
            gap = jnp.zeros(both.shape[:3] + (LANES - 2 * halo,), F32)
            both = jnp.concatenate([both, after, gap, before], axis=dim)
    both = jnp.transpose(both, (0, 2, 1, 3))
    return jnp.concatenate([both, both], axis=2)


def shards(innovations, fractions, cell_index, counts, blocks, u_wind, v_wind, channel_mix):
    slots = innovations.shape[0]
    rows_own = u_wind.shape[1]
    halo = slots - 1
    order = slice(None, None, -1)
    payload = build_payload(innovations[order], fractions[order], cell_index[order], counts[order], blocks[order])
    got = lax.all_to_all(payload, AXES, split_axis=0, concat_axis=0, tiled=True)
    winds = wind_tables(u_wind, v_wind, halo)
    widths = tuple(range(halo, 0, -1))
    forcing, top, bottom = scatter(got, slots, widths, rows_own)
    up, down = ring("lat", False)
    above = lax.ppermute(bottom, "lat", up)
    below = lax.ppermute(top, "lat", down)
    to_left, to_right = lane_pack(forcing, above, below, widths, halo)
    up, down = ring("lon", True)
    west = lax.ppermute(to_right, "lon", up)
    east = lax.ppermute(to_left, "lon", down)
    lat_index = lax.axis_index("lat")
    edge = jnp.stack([lat_index == 0, lat_index == lax.axis_size("lat") - 1]).astype(jnp.int32)
    field = march(edge, forcing, above, below, west, east, winds[0], winds[1], channel_mix.T, widths, halo)
    return field.reshape(VARS, LEV, rows_own, u_wind.shape[2])


def solution(mesh):
    in_specs = (
        P(None, ("lon", "lat"), None, None),
        P(None, ("lon", "lat"), None, None),
        P(None, ("lon", "lat"), None),
        P(None, ("lon", "lat"), None),
        P(None, ("lon", "lat"), None),
        P(None, "lat", "lon"),
        P(None, "lat", "lon"),
        P(),
    )
    out_specs = P(None, None, "lat", "lon")
    return jax.shard_map(shards, mesh=mesh, in_specs=in_specs, out_specs=out_specs, check_vma=False)
```

```python
import functools

import jax
import jax.numpy as jnp
from jax import lax
from jax.experimental import pallas as pl
from jax.experimental.pallas import tpu as pltpu
from jax.sharding import PartitionSpec as P


VARS = 4
LEV = 4
CH = 16
TILE = 16
LANES = 128
KAPPA = 0.125
AXES = ("lon", "lat")
F32 = jnp.float32
BF16 = jnp.bfloat16
CHUNK_A = 4


def offsets_of(widths):
    starts, total = [], 0
    for width in widths:
        starts.append(total)
        total += width
    return starts, total


def pack_rows(slots):
    used = slots * (CH + 3) + 1
    return used, -(-used // 8) * 8


def build_payload(innovations, fractions, cell_index, counts, blocks):
    slots, targets, channels, width = innovations.shape
    tiles = counts.shape[2]
    per_tile = width // tiles
    lane = lax.broadcasted_iota(jnp.int32, (1, 1, width), 2)
    first = lane < per_tile
    count_lane = jnp.where(first, counts[:, :, 0:1], counts[:, :, 1:2])
    block_lane = jnp.where(first, blocks[:, :, 0:1], blocks[:, :, 1:2])
    is_live = (lane & (per_tile - 1)) < count_lane
    values = jnp.where(is_live[:, :, None, :], innovations, jnp.zeros((), BF16))
    row = cell_index >> 4
    column = cell_index & 15
    skewed = (row >> 3) * LANES + ((row + block_lane) & 7) * TILE + column
    used, rows = pack_rows(slots)
    spots = jnp.transpose(blocks, (1, 0, 2)).reshape(targets, 1, slots * tiles)
    spots = jnp.pad(spots, ((0, 0), (0, rows - used), (0, LANES - slots * tiles)))
    return jnp.concatenate(
        [
            jnp.transpose(values, (1, 0, 2, 3)).reshape(targets, slots * channels, width),
            jnp.transpose(fractions, (1, 0, 2, 3)).reshape(targets, slots * 2, width),
            jnp.transpose(skewed, (1, 0, 2)).astype(BF16),
            spots.astype(BF16),
        ],
        axis=1,
    )


def scatter_kernel(slots, batch, widths, early, blocks_ref, got_ref, *rest):
    if widths:
        before_ref, wind_ref, out_ref, left_ref, right_ref, top_ref, bottom_ref = rest[:7]
        rest = rest[7:]
    else:
        out_ref, rest = rest[0], rest[1:]
    below_ref, acc_refs = rest[0], rest[1:]
    step = pl.program_id(0)
    rows_out = out_ref.shape[1]
    base = slots * CH
    tail = got_ref.shape[1] - base

    @pl.when(step == 0)
    def _():
        for acc_ref in acc_refs:
            acc_ref[...] = jnp.zeros_like(acc_ref)

    first = lax.broadcasted_iota(jnp.int32, (CH, LANES), 1) < LANES // 2
    mask_a = jnp.where(first, 1.0, 0.0).astype(BF16)
    mask_b = jnp.where(first, 0.0, 1.0).astype(BF16)
    sixteen = lax.broadcasted_iota(jnp.int32, (TILE, LANES), 0).astype(F32).astype(BF16)
    one_bf, zero_bf = jnp.ones((), BF16), jnp.zeros((), BF16)
    nothing = jnp.zeros((CH, LANES), BF16)

    def one(index, carry):
        sender = step * batch + index
        aux = got_ref[index, pl.ds(base, tail), :].astype(F32)
        major = jnp.floor(aux * (1.0 / TILE))
        minor = aux - TILE * major
        for slot in range(slots):
            value = got_ref[index, pl.ds(slot * CH, CH), :].astype(F32)
            spot = 2 * slots + slot
            by_x = value * aux[2 * slot + 1 : 2 * slot + 2, :]
            frac_y = aux[2 * slot : 2 * slot + 1, :]
            highs, lows = [value.astype(BF16)], [nothing]
            for part in (by_x, value * frac_y, by_x * frac_y):
                high = part.astype(BF16)
                highs.append(high)
                lows.append((part - high.astype(F32)).astype(BF16))
            left = jnp.concatenate(
                [
                    jnp.concatenate([h * m for m in (mask_a, mask_b) for h in highs], axis=0),
                    jnp.concatenate([h * m for m in (mask_a, mask_b) for h in lows], axis=0),
                ],
                axis=1,
            )
            unit = jnp.where(
                sixteen == jnp.broadcast_to(minor[spot : spot + 1], (TILE, LANES)).astype(BF16), one_bf, zero_bf
            )
            group = jnp.broadcast_to(major[spot : spot + 1], (TILE, LANES)).astype(BF16)
            onehot = jnp.concatenate(
                [jnp.where(group == jnp.asarray(k, BF16), unit, zero_bf) for k in range(TILE)], axis=0
            )
            right = jnp.concatenate([onehot, onehot], axis=1)
            sums = lax.dot_general(left, right, (((1,), (1,)), ((), ())), preferred_element_type=F32)
            acc_refs[slot][blocks_ref[sender, 2 * slot]] += sums[: 4 * CH]
            acc_refs[slot][blocks_ref[sender, 2 * slot + 1]] += sums[4 * CH :]
        return carry

    lax.fori_loop(0, batch, one, 0, unroll=4)

    @pl.when(step == pl.num_programs(0) - 1)
    def _():
        lane_group = lax.broadcasted_iota(jnp.int32, (CH, LANES), 1) >> 4
        for slot in range(slots):
            acc_ref = acc_refs[slot]

            def part(number, carry, slot=slot, acc_ref=acc_ref):
                band = number >> 1
                half = number & 1
                straight = [jnp.zeros((CH, LANES), F32)] * 8
                under = [jnp.zeros((CH, LANES), F32)] * 8
                for column in range(8):
                    tile = acc_ref[band * 8 + column, :, pl.ds(pl.multiple_of(half * LANES, LANES), LANES)]
                    a_0, a_x = tile[:CH], tile[CH : 2 * CH]
                    a_y, a_xy = tile[2 * CH : 3 * CH], tile[3 * CH :]
                    x_only, y_only = a_x - a_xy, a_y - a_xy
                    here = a_0 - a_x - y_only + pltpu.roll(x_only, 1, 1)
                    next_row = y_only + pltpu.roll(a_xy, 1, 1)
                    for y in range(8):
                        hit = lane_group == ((y + column) & 7)
                        straight[y] = jnp.where(hit, here, straight[y])
                        under[y] = jnp.where(hit, next_row, under[y])
                for y in range(8):
                    turn = (-16 * y) % LANES
                    row = band * 16 + half * 8 + y
                    out_ref[slot, row] = pltpu.roll(straight[y], turn, 1) if turn else straight[y]
                    below_ref[row] = pltpu.roll(under[y], turn, 1) if turn else under[y]
                return carry

            lax.fori_loop(0, 4, part, 0)
            out_ref[slot, 1:] += below_ref[: rows_out - 1]

        if widths:
            sources = [before_ref.at[k] for k in range(early)]
            sources += [out_ref.at[k] for k in range(len(widths) - 1 - early)] + [wind_ref]
            starts, _ = offsets_of(widths)
            for source, start, width in zip(sources, starts, widths):
                top_ref[start : start + width] = source[:width]
                bottom_ref[start : start + width] = source[rows_out - width :]
            lane = lax.broadcasted_iota(jnp.int32, (CH, LANES), 1)
            per_group = rows_out // GROUPS

            def pack(row, carry):
                to_left = jnp.zeros((CH, LANES), F32)
                to_right = jnp.zeros((CH, LANES), F32)
                for group in range(GROUPS):
                    for source, start, width in zip(sources, starts, widths):
                        value = source[group * per_group + row]
                        begin = group * SPAN + start
                        hit = (lane >= begin) & (lane < begin + width)
                        to_left = jnp.where(hit, pltpu.roll(value, begin, 1) if begin else value, to_left)
                        turn = (begin + width) % LANES
                        to_right = jnp.where(hit, pltpu.roll(value, turn, 1) if turn else value, to_right)
                left_ref[row] = to_left
                right_ref[row] = to_right
                return carry

            lax.fori_loop(0, per_group, pack, 0)


GROUPS = 4
SPAN = LANES // GROUPS


def scatter(got, slots, rows_out, widths=(), before=None, wind=None):
    senders, rows, _ = got.shape
    base = slots * (CH + 3)
    blocks = got[:, base, : 2 * slots].astype(jnp.int32)
    batch = 8
    _, total = offsets_of(widths)

    def whole(shape):
        return pl.BlockSpec(shape, lambda i, b: (0,) * len(shape))

    shapes = [(slots, rows_out, CH, LANES)]
    extra = []
    if widths:
        shapes += [(rows_out // GROUPS, CH, LANES)] * 2 + [(total, CH, LANES)] * 2
        extra = [before, wind]
    return pl.pallas_call(
        functools.partial(scatter_kernel, slots, batch, widths, 0 if before is None else before.shape[0]),
        grid_spec=pltpu.PrefetchScalarGridSpec(
            num_scalar_prefetch=1,
            grid=(senders // batch,),
            in_specs=[pl.BlockSpec((batch, rows, LANES), lambda i, b: (i, 0, 0))] + [whole(e.shape) for e in extra],
            out_specs=[whole(s) for s in shapes],
            scratch_shapes=[pltpu.VMEM((rows_out, CH, LANES), F32)]
            + [pltpu.VMEM((16, 4 * CH, 2 * LANES), F32)] * slots,
        ),
        out_shape=[jax.ShapeDtypeStruct(s, F32) for s in shapes],
        name="scatter",
    )(blocks, got, *extra)


def march_kernel(
    widths, halo, early, edge_ref, first_ref, second_ref, wind_ref, above_ref, below_ref, west_ref, east_ref, mix_ref,
    out_ref, field_ref, extra_ref, mixed_ref, turn_ref,
):
    rows_own = first_ref.shape[1]
    tall = rows_own + 2 * halo
    per_group = west_ref.shape[0]
    starts, total = offsets_of(widths)
    lane = lax.broadcasted_iota(jnp.int32, (CH, LANES), 1)
    main = pl.ds(0, LANES)
    side = pl.ds(LANES, LANES)
    steps = len(widths) - 1
    sources = [first_ref.at[k] for k in range(early)]
    sources += [second_ref.at[k] for k in range(steps - early)] + [wind_ref]

    for slot, (start, width) in enumerate(zip(starts, widths)):
        lo, hi = halo - width, halo + rows_own + width
        extra_ref[slot, hi : hi + 2] = jnp.zeros((2, CH, 2 * LANES), F32)
        extra_ref[slot, lo:halo, :, main] = above_ref[start : start + width]
        extra_ref[slot, halo : halo + rows_own, :, main] = sources[slot][...]
        extra_ref[slot, halo + rows_own : hi, :, main] = below_ref[start : start + width]

    def edge(west, east, group, start, width):
        begin = group * SPAN + start
        turn = (-begin) % LANES
        value = jnp.where(lane < width, pltpu.roll(east, turn, 1) if turn else east, 0.0)
        turn = (LANES - width - begin) % LANES
        return jnp.where(lane >= LANES - width, pltpu.roll(west, turn, 1) if turn else west, value)

    def edges(row, carry):
        west, east = west_ref[row], east_ref[row]
        for group in range(GROUPS):
            for slot, (start, width) in enumerate(zip(starts, widths)):
                extra_ref[slot, halo + group * per_group + row, :, side] = edge(west, east, group, start, width)
        return carry

    lax.fori_loop(0, per_group, edges, 0)
    for slot, (start, width) in enumerate(zip(starts, widths)):
        for i in range(width):
            spot = per_group - width + i
            extra_ref[slot, halo - width + i, :, side] = edge(
                above_ref[total + spot], above_ref[total + per_group + spot], GROUPS - 1, start, width
            )
            extra_ref[slot, halo + rows_own + i, :, side] = edge(
                below_ref[total + i], below_ref[total + per_group + i], 0, start, width
            )

    extra_ref[0, tall:] = jnp.zeros((extra_ref.shape[1] - tall, CH, 2 * LANES), F32)
    field_ref[...] = jnp.zeros_like(field_ref)
    mixed_ref[tall:] = jnp.zeros((mixed_ref.shape[0] - tall, CH, 2 * LANES), F32)
    matrix = mix_ref[...]
    wind = extra_ref.at[steps]
    half = CH // 2

    def mix(source, begin, count):
        for number in range(count):
            rows = pl.ds(begin + 8 * number, 8)
            field = source[rows].reshape(8 * CH, 2 * LANES)
            high = field.astype(BF16)
            low = (field - high.astype(F32)).astype(BF16)
            product = lax.dot_general(
                matrix, jnp.concatenate([high, high, low], axis=0), (((1,), (0,)), ((), ())),
                preferred_element_type=F32,
            )
            mixed_ref[rows] = product.reshape(8, CH, 2 * LANES)

    def twice(value):
        return jnp.concatenate([value, value], axis=0)

    for number in range(steps):
        reach = widths[number]
        source = extra_ref.at[0] if number == 0 else field_ref.at[number % 2]
        target = field_ref.at[(number + 1) % 2]
        begin, end = halo - reach, halo + rows_own + reach
        last = number == steps - 1
        mix(source, begin, -(-(end - begin) // 8))

        def pair(index, carry, target=target, begin=begin, last=last, number=number):
            for offset in range(4):
                row = begin + 1 + 4 * index + offset
                mixed = mixed_ref[row]
                u_half = twice(wind[row, :half]) * 0.5
                result = (1.0 - 4.0 * KAPPA) * mixed
                result = result + pltpu.roll((KAPPA + u_half) * mixed, 2 * LANES - 1, 1)
                result = result + pltpu.roll((KAPPA - u_half) * mixed, 1, 1)
                result = result + (KAPPA + 0.5 * twice(wind[row + 1, half:])) * mixed_ref[row + 1]
                result = result + (KAPPA - 0.5 * twice(wind[row - 1, half:])) * mixed_ref[row - 1]
                if last:
                    turn_ref[row - halo] = result[:, :LANES] + second_ref[steps - early, row - halo]
                else:
                    target[row] = result + extra_ref[number + 1, row]
            return carry

        lax.fori_loop(0, -(-(end - begin - 2) // 4), pair, 0)
        if not last:

            @pl.when(edge_ref[0] == 1)
            def _(target=target):
                target[:halo] = jnp.zeros((halo, CH, 2 * LANES), F32)

            @pl.when(edge_ref[1] == 1)
            def _(target=target):
                target[halo + rows_own : tall] = jnp.zeros((halo, CH, 2 * LANES), F32)

    for channel in range(CH):
        out_ref[channel] = turn_ref[:, channel, :]


def march(edge, first, second, wind, above, below, west, east, mix, widths, halo):
    rows_own = first.shape[1]
    tall = rows_own + 2 * halo
    vmem = pl.BlockSpec(memory_space=pltpu.VMEM)
    return pl.pallas_call(
        functools.partial(march_kernel, widths, halo, first.shape[0]),
        in_specs=[pl.BlockSpec(memory_space=pltpu.SMEM)] + [vmem] * 8,
        out_specs=vmem,
        out_shape=jax.ShapeDtypeStruct((CH, rows_own, LANES), F32),
        scratch_shapes=[
            pltpu.VMEM((2, tall + 8, CH, 2 * LANES), F32),
            pltpu.VMEM((len(widths), tall + 8, CH, 2 * LANES), F32),
            pltpu.VMEM((tall + 8, CH, 2 * LANES), F32),
            pltpu.VMEM((rows_own, CH, LANES), F32),
        ],
        name="march",
    )(edge, first, second, wind, above, below, west, east, mix)


def mix_matrix(channel_mix):
    rounded = lax.reduce_precision(channel_mix.T, 8, 7)
    high = rounded.astype(BF16)
    low = (channel_mix.T - rounded).astype(BF16)
    eye = jnp.eye(8, dtype=BF16)
    return jnp.concatenate([jnp.kron(eye, high), jnp.kron(eye, low), jnp.kron(eye, high)], axis=1)


def ring(axis, wrap):
    count = lax.axis_size(axis)
    up = [(i, (i + 1) % count) for i in range(count if wrap else count - 1)]
    return up, [(j, i) for i, j in up]


def program(innovations, fractions, cell_index, counts, blocks, u_wind, v_wind, channel_mix):
    slots = innovations.shape[0]
    rows_own = u_wind.shape[1]
    halo = slots - 1
    widths = tuple(range(halo, 0, -1)) + (halo,)
    early = CHUNK_A
    got = []
    for low, high in ((slots - early, slots), (0, slots - early)):
        parts = [x[low:high][::-1] for x in (innovations, fractions, cell_index, counts, blocks)]
        payload = build_payload(*parts)
        got.append(lax.all_to_all(payload, AXES, split_axis=0, concat_axis=0, tiled=True))
    u_rows, v_rows = jnp.transpose(u_wind, (1, 0, 2)), jnp.transpose(v_wind, (1, 0, 2))
    wind = jnp.concatenate([u_rows, u_rows, v_rows, v_rows], axis=1)
    (first,) = scatter(got[0], early, rows_own)
    second, to_left, to_right, top, bottom = scatter(got[1], slots - early, rows_own, widths, first, wind)
    up, down = ring("lon", True)
    west = lax.ppermute(to_right, "lon", up)
    east = lax.ppermute(to_left, "lon", down)
    up, down = ring("lat", False)
    above = lax.ppermute(jnp.concatenate([bottom, west, east]), "lat", up)
    below = lax.ppermute(jnp.concatenate([top, west, east]), "lat", down)
    lat_index = lax.axis_index("lat")
    edge = jnp.stack([lat_index == 0, lat_index == lax.axis_size("lat") - 1]).astype(jnp.int32)
    field = march(edge, first, second, wind, above, below, west, east, mix_matrix(channel_mix), widths, halo)
    return field.reshape(VARS, LEV, rows_own, u_wind.shape[2])


def solution(mesh):
    in_specs = (
        P(None, ("lon", "lat"), None, None),
        P(None, ("lon", "lat"), None, None),
        P(None, ("lon", "lat"), None),
        P(None, ("lon", "lat"), None),
        P(None, ("lon", "lat"), None),
        P(None, "lat", "lon"),
        P(None, "lat", "lon"),
        P(),
    )
    out_specs = P(None, None, "lat", "lon")
    return jax.shard_map(program, mesh=mesh, in_specs=in_specs, out_specs=out_specs, check_vma=False)
```

```python
import functools

import jax
import jax.numpy as jnp
from jax import lax
from jax.experimental import pallas as pl
from jax.experimental.pallas import tpu as pltpu
from jax.sharding import PartitionSpec as P


VARS = 4
LEV = 4
CH = 16
TILE = 16
LANES = 128
KAPPA = 0.125
AXES = ("lon", "lat")
F32 = jnp.float32
BF16 = jnp.bfloat16
CHUNK_A = 3


def offsets_of(widths):
    starts, total = [], 0
    for width in widths:
        starts.append(total)
        total += width
    return starts, total


def aux_row(slots, slot):
    return slots * CH + 8 * (slot // 2) + 3 * (slot % 2)


def build_payload(innovations, fractions, cell_index, counts, blocks, every_block):
    slots, targets, channels, width = innovations.shape
    tiles = counts.shape[2]
    per_tile = width // tiles
    lane = lax.broadcasted_iota(jnp.int32, (1, 1, width), 2)
    first = lane < per_tile
    count_lane = jnp.where(first, counts[:, :, 0:1], counts[:, :, 1:2])
    block_lane = jnp.where(first, blocks[:, :, 0:1], blocks[:, :, 1:2])
    is_live = (lane & (per_tile - 1)) < count_lane
    values = jnp.where(is_live[:, :, None, :], innovations, jnp.zeros((), BF16))
    row = cell_index >> 4
    column = cell_index & 15
    skewed = (row >> 3) * LANES + ((row + block_lane) & 7) * TILE + column
    triple = jnp.concatenate([fractions, skewed.astype(BF16)[:, :, None, :]], axis=2)
    pairs = -(-slots // 2)
    triple = jnp.pad(jnp.transpose(triple, (1, 0, 2, 3)), ((0, 0), (0, 2 * pairs - slots), (0, 0), (0, 0)))
    spots = jnp.transpose(every_block, (1, 0, 2)).reshape(targets, 1, 1, -1).astype(BF16)
    spots = jnp.pad(spots, ((0, 0), (0, pairs - 1), (0, 1), (0, LANES - spots.shape[3])))
    aux = jnp.concatenate([triple.reshape(targets, pairs, 6, width), spots], axis=2)
    return jnp.concatenate(
        [
            jnp.transpose(values, (1, 0, 2, 3)).reshape(targets, slots * channels, width),
            aux.reshape(targets, pairs * 8, width),
        ],
        axis=1,
    )


BLOCKS = 16
PARTS = 2
GROUP = 4
UNITS = 2


def group_limit(tiles):
    return (tiles + BLOCKS * (GROUP - 1)) // GROUP


def plan_kernel(slots, spot_row, got_ref, out_ref):
    senders = got_ref.shape[0]
    tiles = 2 * senders
    spots = jnp.transpose(got_ref[:, spot_row, :].astype(F32))
    kind = lax.broadcasted_iota(jnp.int32, (BLOCKS, tiles), 0).astype(F32)
    hits = []
    for slot in range(slots):
        row = jnp.concatenate([spots[2 * slot : 2 * slot + 1], spots[2 * slot + 1 : 2 * slot + 2]], axis=1)
        hits.append(jnp.where(kind == row, 1.0, 0.0))
    hit = jnp.concatenate(hits, axis=0)
    earlier = lax.broadcasted_iota(jnp.int32, (tiles, tiles), 0) < lax.broadcasted_iota(jnp.int32, (tiles, tiles), 1)
    rank = jnp.dot(hit.astype(BF16), jnp.where(earlier, 1.0, 0.0).astype(BF16), preferred_element_type=F32)
    count = jnp.sum(hit, axis=1, keepdims=True)
    groups = jnp.broadcast_to(jnp.floor((count + (GROUP - 1)) * (1.0 / GROUP)), (slots * BLOCKS, LANES))
    above = lax.broadcasted_iota(jnp.int32, (slots * BLOCKS,) * 2, 0)
    across = lax.broadcasted_iota(jnp.int32, (slots * BLOCKS,) * 2, 1)
    lower = jnp.where((above > across) & ((above >> 4) == (across >> 4)), 1.0, 0.0).astype(BF16)
    begin = jnp.dot(lower, groups.astype(BF16), preferred_element_type=F32)
    number = lax.broadcasted_iota(jnp.int32, (BLOCKS, LANES), 1).astype(F32)
    index = lax.broadcasted_iota(jnp.int32, (8, tiles), 1)
    kinds = jnp.where(lax.broadcasted_iota(jnp.int32, (8, tiles), 0) == 0, index, 1).astype(F32).astype(BF16)
    place = lax.broadcasted_iota(jnp.int32, (GROUP * LANES, tiles), 0).astype(F32)
    most = jnp.zeros((1, LANES), F32)
    rows = []
    for slot in range(slots):
        part = slice(slot * BLOCKS, (slot + 1) * BLOCKS)
        start, size = begin[part], groups[part]
        wide = jnp.concatenate([start, start], axis=1)
        fours = jnp.floor(rank[part] * (1.0 / GROUP))
        spot = wide + fours + LANES * (rank[part] - GROUP * fours)
        spot = jnp.sum(hit[part] * spot, axis=0, keepdims=True)
        chosen = jnp.where(place == spot, 1.0, 0.0).astype(BF16)
        order = lax.dot_general(kinds, chosen, (((1,), (1,)), ((), ())), preferred_element_type=F32)
        taken = jnp.zeros((1, LANES), F32)
        for j in range(GROUP):
            tile = order[0:1, j * LANES : (j + 1) * LANES]
            second = jnp.where(tile >= LANES, 1.0, 0.0)
            turned = 1.0 - second if j & 1 else second
            rows.append(tile - LANES * second + LANES * turned)
            taken = taken + order[1:2, j * LANES : (j + 1) * LANES]
        block = jnp.sum(jnp.where(start + size <= number, 1.0, 0.0), axis=0, keepdims=True)
        rows.append(jnp.minimum(block, BLOCKS - 1.0) + BLOCKS * taken)
        most = jnp.maximum(most, start[BLOCKS - 1 :] + size[BLOCKS - 1 :])
    rows += [jnp.zeros((LANES - 1 - len(rows), LANES), F32), most]
    table = jnp.transpose(jnp.concatenate(rows, axis=0))
    out_ref[...] = table[: out_ref.shape[0]].astype(jnp.int32)


def plan(got, slots_all, slots_here):
    senders = got.shape[0]
    spot_row = aux_row(slots_here, 0) + 6
    limit = -(-(group_limit(2 * senders) + 2 * UNITS) // 8) * 8
    return pl.pallas_call(
        functools.partial(plan_kernel, slots_all, spot_row),
        in_specs=[pl.BlockSpec(memory_space=pltpu.VMEM)],
        out_specs=pl.BlockSpec(memory_space=pltpu.VMEM),
        out_shape=jax.ShapeDtypeStruct((limit, LANES), jnp.int32),
        name="plan",
    )(got)


def scatter_kernel(slots, offset, widths, plan_ref, got_ref, *rest):
    late = offset > 0
    if late:
        base_left, base_right = rest[:2]
        rest = rest[2:]
    else:
        wind_ref, rest = rest[0], rest[1:]
    out_ref, left_ref, right_ref, top_ref, bottom_ref, below_ref, held_ref = rest[:7]
    acc_refs = rest[7:]
    rows_out = out_ref.shape[1]

    lane = lax.broadcasted_iota(jnp.int32, (CH, LANES), 1)
    first = lane < LANES // 2
    first_aux = first[:8]
    sixteen = lax.broadcasted_iota(jnp.int32, (TILE, LANES), 0).astype(F32).astype(BF16)
    one_bf, zero_bf = jnp.ones((), BF16), jnp.zeros((), BF16)

    def gather(slot, number, held):
        values, auxes = [], []
        column = 5 * (offset + slot)
        info = plan_ref[number, column + 4]
        for j in range(GROUP):
            entry = plan_ref[number, column + j]
            sender = entry & (LANES - 1)
            turn = (entry & LANES) >> 1
            value = got_ref[sender, pl.ds(slot * CH, CH), :].astype(F32)
            aux = got_ref[sender, pl.ds(aux_row(slots, slot) // 8 * 8, 8), :].astype(F32)
            values.append(pltpu.roll(value, turn, 1))
            auxes.append(pltpu.roll(aux, turn, 1))
        live = (info >> 4) << 6
        for h in range(2):
            value = jnp.where(first, values[2 * h], values[2 * h + 1])
            held[h, :CH] = jnp.where(lane < live - h * LANES, value, 0.0)
            held[h, CH:] = jnp.where(first_aux, auxes[2 * h], auxes[2 * h + 1])

    def unit(slot, held):
        row = aux_row(slots, slot) % 8
        lefts, rights = [], []
        for h in range(2):
            value, aux = held[h, :CH], held[h, CH:]
            major = jnp.floor(aux * (1.0 / TILE))
            minor = aux - TILE * major
            by_x = value * aux[row + 1 : row + 2]
            frac_y = aux[row : row + 1]
            highs, lows = [value.astype(BF16)], []
            for part in (by_x, value * frac_y, by_x * frac_y):
                high = part.astype(BF16)
                highs.append(high)
                lows.append((part - high.astype(F32)).astype(BF16))
            lefts.append(jnp.concatenate(highs + lows, axis=0))
            spot = row + 2
            small = jnp.broadcast_to(minor[spot : spot + 1], (TILE, LANES)).astype(BF16)
            large = jnp.broadcast_to(major[spot : spot + 1], (TILE, LANES)).astype(BF16)
            one_hot = jnp.where(sixteen == small, one_bf, zero_bf)
            rights.append(
                jnp.concatenate(
                    [jnp.where(large == jnp.asarray(k, BF16), one_hot, zero_bf) for k in range(TILE)], axis=0
                )
            )
        return lax.dot_general(
            jnp.concatenate(lefts, axis=1), jnp.concatenate(rights, axis=1), (((1,), (1,)), ((), ())),
            preferred_element_type=F32,
        )

    def add(slot, info, sums):
        block = info & (BLOCKS - 1)
        for part in range(4):
            rows = pl.ds(part * CH, CH)
            total = sums[part * CH : (part + 1) * CH]
            if part:
                total = total + sums[(part + 3) * CH : (part + 4) * CH]
            acc_refs[slot][block, rows] += total

    units = [(slot, k) for k in range(UNITS) for slot in range(slots)]

    def fetch(number):
        for place, (slot, k) in enumerate(units):
            gather(slot, UNITS * number + k, held_ref.at[place])

    def several(number, carry):
        for place, (slot, k) in enumerate(units):
            sums = unit(slot, held_ref.at[place])
            add(slot, plan_ref[UNITS * number + k, 5 * (offset + slot) + 4], sums)
        fetch(number + 1)
        return carry

    for acc_ref in acc_refs:
        acc_ref[...] = jnp.zeros_like(acc_ref)
    fetch(0)
    lax.fori_loop(0, (plan_ref[0, LANES - 1] + UNITS - 1) // UNITS, several, 0)

    lane_group = lane >> 4
    for slot in range(slots):
        acc_ref = acc_refs[slot]

        def part(number, carry, slot=slot, acc_ref=acc_ref):
            band = number >> 1
            half = number & 1
            straight = [jnp.zeros((CH, LANES), F32)] * 8
            under = [jnp.zeros((CH, LANES), F32)] * 8
            for column in range(8):
                tile = acc_ref[band * 8 + column, :, pl.ds(pl.multiple_of(half * LANES, LANES), LANES)]
                a_0, a_x = tile[:CH], tile[CH : 2 * CH]
                a_y, a_xy = tile[2 * CH : 3 * CH], tile[3 * CH :]
                x_only, y_only = a_x - a_xy, a_y - a_xy
                here = a_0 - a_x - y_only + pltpu.roll(x_only, 1, 1)
                next_row = y_only + pltpu.roll(a_xy, 1, 1)
                for y in range(8):
                    hit = lane_group == ((y + column) & 7)
                    straight[y] = jnp.where(hit, here, straight[y])
                    under[y] = jnp.where(hit, next_row, under[y])
            for y in range(8):
                turn = (-16 * y) % LANES
                row = band * 16 + half * 8 + y
                out_ref[slot, row] = pltpu.roll(straight[y], turn, 1) if turn else straight[y]
                below_ref[row] = pltpu.roll(under[y], turn, 1) if turn else under[y]
            return carry

        lax.fori_loop(0, 4, part, 0, unroll=PARTS)
        out_ref[slot, 1:] += below_ref[: rows_out - 1]

    starts, _ = offsets_of(widths)
    jobs = [(out_ref.at[k], starts[offset + k], widths[offset + k]) for k in range(min(slots, len(widths) - 1 - offset))]
    if not late:
        jobs.append((wind_ref, starts[-1], widths[-1]))
    spot = 0
    for source, _, width in jobs:
        top_ref[spot : spot + width] = source[:width]
        bottom_ref[spot : spot + width] = source[rows_out - width :]
        spot += width
    per_group = rows_out // GROUPS

    def pack(row, carry):
        to_left = base_left[row] if late else jnp.zeros((CH, LANES), F32)
        to_right = base_right[row] if late else jnp.zeros((CH, LANES), F32)
        for group in range(GROUPS):
            for source, start, width in jobs:
                value = source[group * per_group + row]
                begin = group * SPAN + start
                hit = (lane >= begin) & (lane < begin + width)
                to_left = jnp.where(hit, pltpu.roll(value, begin, 1) if begin else value, to_left)
                turn = (begin + width) % LANES
                to_right = jnp.where(hit, pltpu.roll(value, turn, 1) if turn else value, to_right)
        left_ref[row] = to_left
        right_ref[row] = to_right
        return carry

    lax.fori_loop(0, per_group, pack, 0)


ROWS = 8
GROUPS = 4
SPAN = LANES // GROUPS


def scatter(got, table, slots, offset, rows_out, widths, *extra):
    carried = sum(widths[offset:-1]) if offset else sum(widths[:slots]) + widths[-1]
    shapes = [(slots, rows_out, CH, LANES)]
    shapes += [(rows_out // GROUPS, CH, LANES)] * 2 + [(carried, CH, LANES)] * 2
    vmem = pl.BlockSpec(memory_space=pltpu.VMEM)
    return pl.pallas_call(
        functools.partial(scatter_kernel, slots, offset, widths),
        in_specs=[pl.BlockSpec(memory_space=pltpu.SMEM), vmem] + [vmem for e in extra],
        out_specs=[vmem for s in shapes],
        scratch_shapes=[
            pltpu.VMEM((rows_out, CH, LANES), F32),
            pltpu.VMEM((UNITS * slots, 2, CH + 8, LANES), F32),
        ]
        + [pltpu.VMEM((BLOCKS, 4 * CH, 2 * LANES), F32)] * slots,
        out_shape=[jax.ShapeDtypeStruct(s, F32) for s in shapes],
        name="scatter",
    )(table, got, *extra)


def march_kernel(
    widths, halo, early, edge_ref, first_ref, second_ref, wind_ref, above_a, above_b, below_a, below_b,
    west_ref, east_ref, mix_ref, out_ref, field_ref, extra_ref, mixed_ref, turn_ref,
):
    rows_own = first_ref.shape[1]
    tall = rows_own + 2 * halo
    per_group = west_ref.shape[0]
    starts, _ = offsets_of(widths)
    lane = lax.broadcasted_iota(jnp.int32, (CH, LANES), 1)
    main = pl.ds(0, LANES)
    side = pl.ds(LANES, LANES)
    steps = len(widths) - 1
    sources = [first_ref.at[k] for k in range(early)]
    sources += [second_ref.at[k] for k in range(steps - early)] + [wind_ref]

    for slot, (start, width) in enumerate(zip(starts, widths)):
        lo, hi = halo - width, halo + rows_own + width
        extra_ref[slot, hi : hi + ROWS] = jnp.zeros((ROWS, CH, 2 * LANES), F32)
        from_a = slot < early or slot == steps
        spot = sum(widths[:early]) if slot == steps else start if from_a else start - sum(widths[:early]) + 2 * halo
        extra_ref[slot, lo:halo, :, main] = (above_a if from_a else above_b)[spot : spot + width]
        extra_ref[slot, halo : halo + rows_own, :, main] = sources[slot][...]
        extra_ref[slot, halo + rows_own : hi, :, main] = (below_a if from_a else below_b)[spot : spot + width]

    def edge(west, east, group, start, width):
        begin = group * SPAN + start
        turn = (-begin) % LANES
        value = jnp.where(lane < width, pltpu.roll(east, turn, 1) if turn else east, 0.0)
        turn = (LANES - width - begin) % LANES
        return jnp.where(lane >= LANES - width, pltpu.roll(west, turn, 1) if turn else west, value)

    def edges(row, carry):
        west, east = west_ref[row], east_ref[row]
        for group in range(GROUPS):
            for slot, (start, width) in enumerate(zip(starts, widths)):
                extra_ref[slot, halo + group * per_group + row, :, side] = edge(west, east, group, start, width)
        return carry

    lax.fori_loop(0, per_group, edges, 0)
    for slot, (start, width) in enumerate(zip(starts, widths)):
        for i in range(width):
            spot = halo - width + i
            extra_ref[slot, spot, :, side] = edge(above_b[spot], above_b[spot + halo], GROUPS - 1, start, width)
            extra_ref[slot, halo + rows_own + i, :, side] = edge(below_b[i], below_b[halo + i], 0, start, width)

    extra_ref[0, tall:] = jnp.zeros((extra_ref.shape[1] - tall, CH, 2 * LANES), F32)
    field_ref[...] = jnp.zeros_like(field_ref)
    mixed_ref[tall:] = jnp.zeros((mixed_ref.shape[0] - tall, CH, 2 * LANES), F32)
    matrix = mix_ref[...]
    wind = extra_ref.at[steps]
    half = CH // 2

    def mix(source, begin, count):
        for number in range(count):
            rows = pl.ds(begin + 8 * number, 8)
            field = source[rows].reshape(8 * CH, 2 * LANES)
            high = field.astype(BF16)
            low = (field - high.astype(F32)).astype(BF16)
            product = lax.dot_general(
                matrix, jnp.concatenate([high, high, low], axis=0), (((1,), (0,)), ((), ())),
                preferred_element_type=F32,
            )
            mixed_ref[rows] = product.reshape(8, CH, 2 * LANES)

    def twice(value):
        return jnp.concatenate([value, value], axis=0)

    for number in range(steps):
        reach = widths[number]
        source = extra_ref.at[0] if number == 0 else field_ref.at[number % 2]
        target = field_ref.at[(number + 1) % 2]
        begin, end = halo - reach, halo + rows_own + reach
        last = number == steps - 1
        mix(source, begin, -(-(end - begin) // 8))

        def pair(index, carry, target=target, begin=begin, last=last, number=number):
            for offset in range(ROWS):
                row = begin + 1 + ROWS * index + offset
                mixed = mixed_ref[row]
                u_half = twice(wind[row, :half]) * 0.5
                result = (1.0 - 4.0 * KAPPA) * mixed
                result = result + pltpu.roll((KAPPA + u_half) * mixed, 2 * LANES - 1, 1)
                result = result + pltpu.roll((KAPPA - u_half) * mixed, 1, 1)
                result = result + (KAPPA + 0.5 * twice(wind[row + 1, half:])) * mixed_ref[row + 1]
                result = result + (KAPPA - 0.5 * twice(wind[row - 1, half:])) * mixed_ref[row - 1]
                if last:
                    turn_ref[row - halo] = result[:, :LANES] + second_ref[steps - early, row - halo]
                else:
                    target[row] = result + extra_ref[number + 1, row]
            return carry

        lax.fori_loop(0, -(-(end - begin - 2) // ROWS), pair, 0)
        if not last:

            @pl.when(edge_ref[0] == 1)
            def _(target=target):
                target[:halo] = jnp.zeros((halo, CH, 2 * LANES), F32)

            @pl.when(edge_ref[1] == 1)
            def _(target=target):
                target[halo + rows_own : tall] = jnp.zeros((halo, CH, 2 * LANES), F32)

    for channel in range(CH):
        out_ref[channel] = turn_ref[:, channel, :]


def march(edge, first, second, wind, above, below, west, east, mix, widths, halo):
    rows_own = first.shape[1]
    tall = rows_own + 2 * halo
    vmem = pl.BlockSpec(memory_space=pltpu.VMEM)
    return pl.pallas_call(
        functools.partial(march_kernel, widths, halo, first.shape[0]),
        in_specs=[pl.BlockSpec(memory_space=pltpu.SMEM)] + [vmem] * 10,
        out_specs=vmem,
        out_shape=jax.ShapeDtypeStruct((CH, rows_own, LANES), F32),
        scratch_shapes=[
            pltpu.VMEM((2, tall + 8, CH, 2 * LANES), F32),
            pltpu.VMEM((len(widths), tall + 8, CH, 2 * LANES), F32),
            pltpu.VMEM((tall + 8, CH, 2 * LANES), F32),
            pltpu.VMEM((rows_own, CH, LANES), F32),
        ],
        name="march",
    )(edge, first, second, wind, *above, *below, west, east, mix)


def mix_matrix(channel_mix):
    rounded = lax.reduce_precision(channel_mix.T, 8, 7)
    high = rounded.astype(BF16)
    low = (channel_mix.T - rounded).astype(BF16)
    eye = jnp.eye(8, dtype=BF16)
    return jnp.concatenate([jnp.kron(eye, high), jnp.kron(eye, low), jnp.kron(eye, high)], axis=1)


def ring(axis, wrap):
    count = lax.axis_size(axis)
    up = [(i, (i + 1) % count) for i in range(count if wrap else count - 1)]
    return up, [(j, i) for i, j in up]


def program(innovations, fractions, cell_index, counts, blocks, u_wind, v_wind, channel_mix):
    slots = innovations.shape[0]
    rows_own = u_wind.shape[1]
    halo = slots - 1
    widths = tuple(range(halo, 0, -1)) + (halo,)
    early = CHUNK_A
    got = []
    for name, low, high in (("move_a", slots - early, slots), ("move_b", 0, slots - early)):
        parts = [x[low:high][::-1] for x in (innovations, fractions, cell_index, counts, blocks)]
        payload = build_payload(*parts, blocks[::-1] if name == "move_a" else parts[4])
        got.append(lax.all_to_all(payload, AXES, split_axis=0, concat_axis=0, tiled=True))
    u_rows, v_rows = jnp.transpose(u_wind, (1, 0, 2)), jnp.transpose(v_wind, (1, 0, 2))
    wind = jnp.concatenate([u_rows, u_rows, v_rows, v_rows], axis=1)
    table = plan(got[0], slots, early)
    first, left_a, right_a, top_a, bottom_a = scatter(got[0], table, early, 0, rows_own, widths, wind)
    up, down = ring("lat", False)
    above_a, below_a = lax.ppermute(bottom_a, "lat", up), lax.ppermute(top_a, "lat", down)
    second, to_left, to_right, top_b, bottom_b = scatter(
        got[1], table, slots - early, early, rows_own, widths, left_a, right_a
    )
    per_group = to_left.shape[0]
    up, down = ring("lon", True)
    west = lax.ppermute(to_right, "lon", up)
    east = lax.ppermute(to_left, "lon", down)
    up, down = ring("lat", False)
    last_up = jnp.concatenate([west[per_group - halo :], east[per_group - halo :], bottom_b])
    last_down = jnp.concatenate([west[:halo], east[:halo], top_b])
    above = [above_a, lax.ppermute(last_up, "lat", up)]
    below = [below_a, lax.ppermute(last_down, "lat", down)]
    lat_index = lax.axis_index("lat")
    edge = jnp.stack([lat_index == 0, lat_index == lax.axis_size("lat") - 1]).astype(jnp.int32)
    field = march(edge, first, second, wind, above, below, west, east, mix_matrix(channel_mix), widths, halo)
    return field.reshape(VARS, LEV, rows_own, u_wind.shape[2])


def solution(mesh):
    in_specs = (
        P(None, ("lon", "lat"), None, None),
        P(None, ("lon", "lat"), None, None),
        P(None, ("lon", "lat"), None),
        P(None, ("lon", "lat"), None),
        P(None, ("lon", "lat"), None),
        P(None, "lat", "lon"),
        P(None, "lat", "lon"),
        P(),
    )
    out_specs = P(None, None, "lat", "lon")
    return jax.shard_map(program, mesh=mesh, in_specs=in_specs, out_specs=out_specs, check_vma=False)
```

```python
import functools

import jax
import jax.numpy as jnp
from jax import lax
from jax.experimental import pallas as pl
from jax.experimental.pallas import tpu as pltpu
from jax.sharding import PartitionSpec as P


VARS = 4
LEV = 4
CH = 16
TILE = 16
LANES = 128
KAPPA = 0.125
AXES = ("lon", "lat")
F32 = jnp.float32
BF16 = jnp.bfloat16
CHUNK_A = 3


def offsets_of(widths):
    starts, total = [], 0
    for width in widths:
        starts.append(total)
        total += width
    return starts, total


def aux_row(slots, slot):
    return slots * CH + 8 * (slot // 2) + 3 * (slot % 2)


def build_payload(innovations, fractions, cell_index, counts, blocks, every_block):
    slots, targets, channels, width = innovations.shape
    tiles = counts.shape[2]
    per_tile = width // tiles
    lane = lax.broadcasted_iota(jnp.int32, (1, 1, width), 2)
    first = lane < per_tile
    count_lane = jnp.where(first, counts[:, :, 0:1], counts[:, :, 1:2])
    block_lane = jnp.where(first, blocks[:, :, 0:1], blocks[:, :, 1:2])
    is_live = (lane & (per_tile - 1)) < count_lane
    values = jnp.where(is_live[:, :, None, :], innovations, jnp.zeros((), BF16))
    row = cell_index >> 4
    column = cell_index & 15
    skewed = (row >> 3) * LANES + ((row + block_lane) & 7) * TILE + column
    triple = jnp.concatenate([fractions, skewed.astype(BF16)[:, :, None, :]], axis=2)
    pairs = -(-slots // 2)
    triple = jnp.pad(jnp.transpose(triple, (1, 0, 2, 3)), ((0, 0), (0, 2 * pairs - slots), (0, 0), (0, 0)))
    spots = jnp.transpose(every_block, (1, 0, 2)).reshape(targets, 1, 1, -1).astype(BF16)
    spots = jnp.pad(spots, ((0, 0), (0, pairs - 1), (0, 1), (0, LANES - spots.shape[3])))
    aux = jnp.concatenate([triple.reshape(targets, pairs, 6, width), spots], axis=2)
    return jnp.concatenate(
        [
            jnp.transpose(values, (1, 0, 2, 3)).reshape(targets, slots * channels, width),
            aux.reshape(targets, pairs * 8, width),
        ],
        axis=1,
    )


BLOCKS = 16
PARTS = 4
GROUP = 4
UNITS = 4


def group_limit(tiles):
    return (tiles + BLOCKS * (GROUP - 1)) // GROUP


def plan_kernel(slots, spot_row, got_ref, out_ref):
    senders = got_ref.shape[0]
    tiles = 2 * senders
    spots = jnp.transpose(got_ref[:, spot_row, :].astype(F32))
    kind = lax.broadcasted_iota(jnp.int32, (BLOCKS, tiles), 0).astype(F32)
    hits = []
    for slot in range(slots):
        row = jnp.concatenate([spots[2 * slot : 2 * slot + 1], spots[2 * slot + 1 : 2 * slot + 2]], axis=1)
        hits.append(jnp.where(kind == row, 1.0, 0.0))
    hit = jnp.concatenate(hits, axis=0)
    earlier = lax.broadcasted_iota(jnp.int32, (tiles, tiles), 0) < lax.broadcasted_iota(jnp.int32, (tiles, tiles), 1)
    rank = jnp.dot(hit.astype(BF16), jnp.where(earlier, 1.0, 0.0).astype(BF16), preferred_element_type=F32)
    count = jnp.sum(hit, axis=1, keepdims=True)
    groups = jnp.broadcast_to(jnp.floor((count + (GROUP - 1)) * (1.0 / GROUP)), (slots * BLOCKS, LANES))
    above = lax.broadcasted_iota(jnp.int32, (slots * BLOCKS,) * 2, 0)
    across = lax.broadcasted_iota(jnp.int32, (slots * BLOCKS,) * 2, 1)
    lower = jnp.where((above > across) & ((above >> 4) == (across >> 4)), 1.0, 0.0).astype(BF16)
    begin = jnp.dot(lower, groups.astype(BF16), preferred_element_type=F32)
    number = lax.broadcasted_iota(jnp.int32, (BLOCKS, LANES), 1).astype(F32)
    index = lax.broadcasted_iota(jnp.int32, (8, tiles), 1)
    kinds = jnp.where(lax.broadcasted_iota(jnp.int32, (8, tiles), 0) == 0, index, 1).astype(F32).astype(BF16)
    place = lax.broadcasted_iota(jnp.int32, (GROUP * LANES, tiles), 0).astype(F32)
    most = jnp.zeros((1, LANES), F32)
    rows = []
    for slot in range(slots):
        part = slice(slot * BLOCKS, (slot + 1) * BLOCKS)
        start, size = begin[part], groups[part]
        wide = jnp.concatenate([start, start], axis=1)
        fours = jnp.floor(rank[part] * (1.0 / GROUP))
        spot = wide + fours + LANES * (rank[part] - GROUP * fours)
        spot = jnp.sum(hit[part] * spot, axis=0, keepdims=True)
        chosen = jnp.where(place == spot, 1.0, 0.0).astype(BF16)
        order = lax.dot_general(kinds, chosen, (((1,), (1,)), ((), ())), preferred_element_type=F32)
        taken = jnp.zeros((1, LANES), F32)
        for j in range(GROUP):
            tile = order[0:1, j * LANES : (j + 1) * LANES]
            second = jnp.where(tile >= LANES, 1.0, 0.0)
            turned = 1.0 - second if j & 1 else second
            rows.append(tile - LANES * second + LANES * turned)
            taken = taken + order[1:2, j * LANES : (j + 1) * LANES]
        block = jnp.sum(jnp.where(start + size <= number, 1.0, 0.0), axis=0, keepdims=True)
        rows.append(jnp.minimum(block, BLOCKS - 1.0) + BLOCKS * taken)
        most = jnp.maximum(most, start[BLOCKS - 1 :] + size[BLOCKS - 1 :])
    rows += [jnp.zeros((LANES - 1 - len(rows), LANES), F32), most]
    table = jnp.transpose(jnp.concatenate(rows, axis=0))
    out_ref[...] = table[: out_ref.shape[0]].astype(jnp.int32)


def plan(got, slots_all, slots_here):
    senders = got.shape[0]
    spot_row = aux_row(slots_here, 0) + 6
    limit = -(-(group_limit(2 * senders) + 2 * UNITS) // 8) * 8
    return pl.pallas_call(
        functools.partial(plan_kernel, slots_all, spot_row),
        in_specs=[pl.BlockSpec(memory_space=pltpu.VMEM)],
        out_specs=pl.BlockSpec(memory_space=pltpu.VMEM),
        out_shape=jax.ShapeDtypeStruct((limit, LANES), jnp.int32),
        name="plan",
    )(got)


def scatter_kernel(slots, offset, widths, plan_ref, got_ref, *rest):
    late = offset > 0
    extra_ref, out_ref, pack_ref, top_ref, bottom_ref, below_ref, held_ref = rest[:7]
    acc_refs = rest[7:]
    rows_out = out_ref.shape[1]

    lane = lax.broadcasted_iota(jnp.int32, (CH, LANES), 1)
    first = lane < LANES // 2
    first_aux = first[:8]
    sixteen = lax.broadcasted_iota(jnp.int32, (TILE, LANES), 0).astype(F32).astype(BF16)
    one_bf, zero_bf = jnp.ones((), BF16), jnp.zeros((), BF16)

    def gather(slot, number, held):
        values, auxes = [], []
        column = 5 * (offset + slot)
        info = plan_ref[number, column + 4]
        for j in range(GROUP):
            entry = plan_ref[number, column + j]
            sender = entry & (LANES - 1)
            turn = (entry & LANES) >> 1
            value = got_ref[sender, pl.ds(slot * CH, CH), :].astype(F32)
            aux = got_ref[sender, pl.ds(aux_row(slots, slot) // 8 * 8, 8), :].astype(F32)
            values.append(pltpu.roll(value, turn, 1))
            auxes.append(pltpu.roll(aux, turn, 1))
        live = (info >> 4) << 6
        for h in range(2):
            value = jnp.where(first, values[2 * h], values[2 * h + 1])
            held[h, :CH] = jnp.where(lane < live - h * LANES, value, 0.0)
            held[h, CH:] = jnp.where(first_aux, auxes[2 * h], auxes[2 * h + 1])

    def unit(slot, held):
        row = aux_row(slots, slot) % 8
        lefts, rights = [], []
        for h in range(2):
            value, aux = held[h, :CH], held[h, CH:]
            major = jnp.floor(aux * (1.0 / TILE))
            minor = aux - TILE * major
            by_x = value * aux[row + 1 : row + 2]
            frac_y = aux[row : row + 1]
            highs, lows = [value.astype(BF16)], []
            for part in (by_x, value * frac_y, by_x * frac_y):
                high = part.astype(BF16)
                highs.append(high)
                lows.append((part - high.astype(F32)).astype(BF16))
            lefts.append(jnp.concatenate(highs + lows, axis=0))
            spot = row + 2
            small = jnp.broadcast_to(minor[spot : spot + 1], (TILE, LANES)).astype(BF16)
            large = jnp.broadcast_to(major[spot : spot + 1], (TILE, LANES)).astype(BF16)
            one_hot = jnp.where(sixteen == small, one_bf, zero_bf)
            rights.append(
                jnp.concatenate(
                    [jnp.where(large == jnp.asarray(k, BF16), one_hot, zero_bf) for k in range(TILE)], axis=0
                )
            )
        return lax.dot_general(
            jnp.concatenate(lefts, axis=1), jnp.concatenate(rights, axis=1), (((1,), (1,)), ((), ())),
            preferred_element_type=F32,
        )

    def add(slot, info, sums):
        block = info & (BLOCKS - 1)
        for part in range(4):
            rows = pl.ds(part * CH, CH)
            total = sums[part * CH : (part + 1) * CH]
            if part:
                total = total + sums[(part + 3) * CH : (part + 4) * CH]
            acc_refs[slot][block, rows] += total

    units = [(slot, k) for k in range(UNITS) for slot in range(slots)]

    def fetch(number):
        for place, (slot, k) in enumerate(units):
            gather(slot, UNITS * number + k, held_ref.at[place])

    def several(number, carry):
        for place, (slot, k) in enumerate(units):
            sums = unit(slot, held_ref.at[place])
            add(slot, plan_ref[UNITS * number + k, 5 * (offset + slot) + 4], sums)
        fetch(number + 1)
        return carry

    for acc_ref in acc_refs:
        acc_ref[...] = jnp.zeros_like(acc_ref)
    fetch(0)
    lax.fori_loop(0, (plan_ref[0, LANES - 1] + UNITS - 1) // UNITS, several, 0)

    lane_group = lane >> 4
    for slot in range(slots):
        acc_ref = acc_refs[slot]

        def part(number, carry, slot=slot, acc_ref=acc_ref):
            band = number >> 1
            half = number & 1
            straight = [jnp.zeros((CH, LANES), F32)] * 8
            under = [jnp.zeros((CH, LANES), F32)] * 8
            for column in range(8):
                tile = acc_ref[band * 8 + column, :, pl.ds(pl.multiple_of(half * LANES, LANES), LANES)]
                a_0, a_x = tile[:CH], tile[CH : 2 * CH]
                a_y, a_xy = tile[2 * CH : 3 * CH], tile[3 * CH :]
                x_only, y_only = a_x - a_xy, a_y - a_xy
                here = a_0 - a_x - y_only + pltpu.roll(x_only, 1, 1)
                next_row = y_only + pltpu.roll(a_xy, 1, 1)
                for y in range(8):
                    hit = lane_group == ((y + column) & 7)
                    straight[y] = jnp.where(hit, here, straight[y])
                    under[y] = jnp.where(hit, next_row, under[y])
            for y in range(8):
                turn = (-16 * y) % LANES
                row = band * 16 + half * 8 + y
                out_ref[slot, row] = pltpu.roll(straight[y], turn, 1) if turn else straight[y]
                below_ref[row] = pltpu.roll(under[y], turn, 1) if turn else under[y]
            return carry

        lax.fori_loop(0, 4, part, 0, unroll=PARTS)
        out_ref[slot, 1:] += below_ref[: rows_out - 1]

    starts, _ = offsets_of(widths)
    jobs = [(out_ref.at[k], starts[offset + k], widths[offset + k]) for k in range(min(slots, len(widths) - 1 - offset))]
    if not late:
        jobs.append((extra_ref, starts[-1], widths[-1]))
    spot = 0
    for source, _, width in jobs:
        top_ref[spot : spot + width] = source[:width]
        bottom_ref[spot : spot + width] = source[rows_out - width :]
        spot += width
    per_group = rows_out // GROUPS

    def pack(row, carry):
        total = extra_ref[row] if late else jnp.zeros((CH, LANES), F32)
        for group in range(GROUPS):
            for source, start, width in jobs:
                value = source[group * per_group + row]
                begin = group * SPAN + 2 * start
                hit = (lane >= begin) & (lane < begin + 2 * width)
                turn = (begin + width) % LANES
                total = jnp.where(hit, pltpu.roll(value, turn, 1) if turn else value, total)
        pack_ref[row] = total
        return carry

    lax.fori_loop(0, per_group, pack, 0, unroll=4)


ROWS = 8
GROUPS = 2
SPAN = LANES // GROUPS


def scatter(got, table, slots, offset, rows_out, widths, *extra):
    carried = sum(widths[offset:-1]) if offset else sum(widths[:slots]) + widths[-1]
    shapes = [(slots, rows_out, CH, LANES)]
    shapes += [(rows_out // GROUPS, CH, LANES)] + [(carried, CH, LANES)] * 2
    vmem = pl.BlockSpec(memory_space=pltpu.VMEM)
    return pl.pallas_call(
        functools.partial(scatter_kernel, slots, offset, widths),
        in_specs=[pl.BlockSpec(memory_space=pltpu.SMEM), vmem] + [vmem for e in extra],
        out_specs=[vmem for s in shapes],
        scratch_shapes=[
            pltpu.VMEM((rows_out, CH, LANES), F32),
            pltpu.VMEM((UNITS * slots, 2, CH + 8, LANES), F32),
        ]
        + [pltpu.VMEM((BLOCKS, 4 * CH, 2 * LANES), F32)] * slots,
        out_shape=[jax.ShapeDtypeStruct(s, F32) for s in shapes],
        name="scatter",
    )(table, got, *extra)


def march_kernel(
    widths, halo, early, edge_ref, first_ref, second_ref, wind_ref, above_a, above_b, below_a, below_b,
    ends_ref, mix_ref, out_ref, field_ref, extra_ref, mixed_ref, turn_ref,
):
    rows_own = first_ref.shape[1]
    tall = rows_own + 2 * halo
    per_group = ends_ref.shape[0]
    starts, _ = offsets_of(widths)
    lane = lax.broadcasted_iota(jnp.int32, (CH, LANES), 1)
    main = pl.ds(0, LANES)
    side = pl.ds(LANES, LANES)
    steps = len(widths) - 1
    sources = [first_ref.at[k] for k in range(early)]
    sources += [second_ref.at[k] for k in range(steps - early)] + [wind_ref]

    for slot, (start, width) in enumerate(zip(starts, widths)):
        lo, hi = halo - width, halo + rows_own + width
        extra_ref[slot, hi : hi + ROWS] = jnp.zeros((ROWS, CH, 2 * LANES), F32)
        from_a = slot < early or slot == steps
        spot = sum(widths[:early]) if slot == steps else start if from_a else start - sum(widths[:early]) + halo
        extra_ref[slot, lo:halo, :, main] = (above_a if from_a else above_b)[spot : spot + width]
        extra_ref[slot, halo : halo + rows_own, :, main] = sources[slot][...]
        extra_ref[slot, halo + rows_own : hi, :, main] = (below_a if from_a else below_b)[spot : spot + width]

    def edge(ends, group, start, width):
        turn = -(group * SPAN + 2 * start + width) % LANES
        kept = (lane < width) | (lane >= LANES - width)
        return jnp.where(kept, pltpu.roll(ends, turn, 1) if turn else ends, 0.0)

    def edges(row, carry):
        ends = ends_ref[row]
        for group in range(GROUPS):
            for slot, (start, width) in enumerate(zip(starts, widths)):
                extra_ref[slot, halo + group * per_group + row, :, side] = edge(ends, group, start, width)
        return carry

    lax.fori_loop(0, per_group, edges, 0, unroll=4)
    for slot, (start, width) in enumerate(zip(starts, widths)):
        for i in range(width):
            spot = halo - width + i
            extra_ref[slot, spot, :, side] = edge(above_b[spot], GROUPS - 1, start, width)
            extra_ref[slot, halo + rows_own + i, :, side] = edge(below_b[i], 0, start, width)

    extra_ref[0, tall:] = jnp.zeros((extra_ref.shape[1] - tall, CH, 2 * LANES), F32)
    field_ref[...] = jnp.zeros_like(field_ref)
    mixed_ref[tall:] = jnp.zeros((mixed_ref.shape[0] - tall, CH, 2 * LANES), F32)
    matrix = mix_ref[...]
    wind = extra_ref.at[steps]
    half = CH // 2

    def mix(source, begin, count):
        for number in range(count):
            rows = pl.ds(begin + 8 * number, 8)
            field = source[rows].reshape(8 * CH, 2 * LANES)
            high = field.astype(BF16)
            low = (field - high.astype(F32)).astype(BF16)
            product = lax.dot_general(
                matrix, jnp.concatenate([high, high, low], axis=0), (((1,), (0,)), ((), ())),
                preferred_element_type=F32,
            )
            mixed_ref[rows] = product.reshape(8, CH, 2 * LANES)

    def twice(value):
        return jnp.concatenate([value, value], axis=0)

    for number in range(steps):
        reach = widths[number]
        source = extra_ref.at[0] if number == 0 else field_ref.at[number % 2]
        target = field_ref.at[(number + 1) % 2]
        begin, end = halo - reach, halo + rows_own + reach
        last = number == steps - 1
        mix(source, begin, -(-(end - begin) // 8))

        def pair(index, carry, target=target, begin=begin, last=last, number=number):
            for offset in range(ROWS):
                row = begin + 1 + ROWS * index + offset
                mixed = mixed_ref[row]
                u_half = twice(wind[row, :half]) * 0.5
                result = (1.0 - 4.0 * KAPPA) * mixed
                result = result + pltpu.roll((KAPPA + u_half) * mixed, 2 * LANES - 1, 1)
                result = result + pltpu.roll((KAPPA - u_half) * mixed, 1, 1)
                result = result + (KAPPA + 0.5 * twice(wind[row + 1, half:])) * mixed_ref[row + 1]
                result = result + (KAPPA - 0.5 * twice(wind[row - 1, half:])) * mixed_ref[row - 1]
                if last:
                    turn_ref[row - halo] = result[:, :LANES] + second_ref[steps - early, row - halo]
                else:
                    target[row] = result + extra_ref[number + 1, row]
            return carry

        lax.fori_loop(0, -(-(end - begin - 2) // ROWS), pair, 0)
        if not last:

            @pl.when(edge_ref[0] == 1)
            def _(target=target):
                target[:halo] = jnp.zeros((halo, CH, 2 * LANES), F32)

            @pl.when(edge_ref[1] == 1)
            def _(target=target):
                target[halo + rows_own : tall] = jnp.zeros((halo, CH, 2 * LANES), F32)

    for channel in range(CH):
        out_ref[channel] = turn_ref[:, channel, :]


def march(edge, first, second, wind, above, below, ends, mix, widths, halo):
    rows_own = first.shape[1]
    tall = rows_own + 2 * halo
    vmem = pl.BlockSpec(memory_space=pltpu.VMEM)
    return pl.pallas_call(
        functools.partial(march_kernel, widths, halo, first.shape[0]),
        in_specs=[pl.BlockSpec(memory_space=pltpu.SMEM)] + [vmem] * 9,
        out_specs=vmem,
        out_shape=jax.ShapeDtypeStruct((CH, rows_own, LANES), F32),
        scratch_shapes=[
            pltpu.VMEM((2, tall + 8, CH, 2 * LANES), F32),
            pltpu.VMEM((len(widths), tall + 8, CH, 2 * LANES), F32),
            pltpu.VMEM((tall + 8, CH, 2 * LANES), F32),
            pltpu.VMEM((rows_own, CH, LANES), F32),
        ],
        name="march",
    )(edge, first, second, wind, *above, *below, ends, mix)


def west_lanes(widths):
    lane = lax.broadcasted_iota(jnp.int32, (1, 1, LANES), 2) % SPAN
    starts, _ = offsets_of(widths)
    found = lane < 0
    for start, width in zip(starts, widths):
        found = found | ((lane >= 2 * start) & (lane < 2 * start + width))
    return found


def mix_matrix(channel_mix):
    rounded = lax.reduce_precision(channel_mix.T, 8, 7)
    high = rounded.astype(BF16)
    low = (channel_mix.T - rounded).astype(BF16)
    eye = jnp.eye(8, dtype=BF16)
    return jnp.concatenate([jnp.kron(eye, high), jnp.kron(eye, low), jnp.kron(eye, high)], axis=1)


def ring(axis, wrap):
    count = lax.axis_size(axis)
    up = [(i, (i + 1) % count) for i in range(count if wrap else count - 1)]
    return up, [(j, i) for i, j in up]


def program(innovations, fractions, cell_index, counts, blocks, u_wind, v_wind, channel_mix):
    slots = innovations.shape[0]
    rows_own = u_wind.shape[1]
    halo = slots - 1
    widths = tuple(range(halo, 0, -1)) + (halo,)
    early = CHUNK_A
    got = []
    for name, low, high in (("move_a", slots - early, slots), ("move_b", 0, slots - early)):
        parts = [x[low:high][::-1] for x in (innovations, fractions, cell_index, counts, blocks)]
        payload = build_payload(*parts, blocks[::-1] if name == "move_a" else parts[4])
        got.append(lax.all_to_all(payload, AXES, split_axis=0, concat_axis=0, tiled=True))
    u_rows, v_rows = jnp.transpose(u_wind, (1, 0, 2)), jnp.transpose(v_wind, (1, 0, 2))
    wind = jnp.concatenate([u_rows, u_rows, v_rows, v_rows], axis=1)
    table = plan(got[0], slots, early)
    first, pack_a, top_a, bottom_a = scatter(got[0], table, early, 0, rows_own, widths, wind)
    up, down = ring("lat", False)
    above_a, below_a = lax.ppermute(bottom_a, "lat", up), lax.ppermute(top_a, "lat", down)
    second, pack, top_b, bottom_b = scatter(got[1], table, slots - early, early, rows_own, widths, pack_a)
    around, back = ring("lon", True)
    west = lax.ppermute(pack, "lon", around)
    east = lax.ppermute(pack, "lon", back)
    ends = jnp.where(west_lanes(widths), west, east)
    last_up = jnp.concatenate([ends[-halo:], bottom_b])
    last_down = jnp.concatenate([ends[:halo], top_b])
    above = [above_a, lax.ppermute(last_up, "lat", up)]
    below = [below_a, lax.ppermute(last_down, "lat", down)]
    lat_index = lax.axis_index("lat")
    edge = jnp.stack([lat_index == 0, lat_index == lax.axis_size("lat") - 1]).astype(jnp.int32)
    field = march(edge, first, second, wind, above, below, ends, mix_matrix(channel_mix), widths, halo)
    return field.reshape(VARS, LEV, rows_own, u_wind.shape[2])


def solution(mesh):
    in_specs = (
        P(None, ("lon", "lat"), None, None),
        P(None, ("lon", "lat"), None, None),
        P(None, ("lon", "lat"), None),
        P(None, ("lon", "lat"), None),
        P(None, ("lon", "lat"), None),
        P(None, "lat", "lon"),
        P(None, "lat", "lon"),
        P(),
    )
    out_specs = P(None, None, "lat", "lon")
    return jax.shard_map(program, mesh=mesh, in_specs=in_specs, out_specs=out_specs, check_vma=False)
```

```python
import functools

import jax
import jax.numpy as jnp
from jax import lax
from jax.experimental import pallas as pl
from jax.experimental.pallas import tpu as pltpu
from jax.sharding import PartitionSpec as P


VARS = 4
LEV = 4
CH = 16
TILE = 16
LANES = 128
KAPPA = 0.125
AXES = ("lon", "lat")
F32 = jnp.float32
BF16 = jnp.bfloat16
CHUNK_A = 3


def offsets_of(widths):
    starts, total = [], 0
    for width in widths:
        starts.append(total)
        total += width
    return starts, total


def aux_row(slots, slot):
    return slots * CH + 8 * (slot // 2) + 3 * (slot % 2)


def build_payload(innovations, fractions, cell_index, counts, blocks, every_block):
    slots, targets, channels, width = innovations.shape
    tiles = counts.shape[2]
    per_tile = width // tiles
    lane = lax.broadcasted_iota(jnp.int32, (1, 1, width), 2)
    first = lane < per_tile
    count_lane = jnp.where(first, counts[:, :, 0:1], counts[:, :, 1:2])
    block_lane = jnp.where(first, blocks[:, :, 0:1], blocks[:, :, 1:2])
    is_live = (lane & (per_tile - 1)) < count_lane
    values = jnp.where(is_live[:, :, None, :], innovations, jnp.zeros((), BF16))
    row = cell_index >> 4
    column = cell_index & 15
    skewed = (row >> 3) * LANES + ((row + block_lane) & 7) * TILE + column
    triple = jnp.concatenate([fractions, skewed.astype(BF16)[:, :, None, :]], axis=2)
    pairs = -(-slots // 2)
    triple = jnp.pad(jnp.transpose(triple, (1, 0, 2, 3)), ((0, 0), (0, 2 * pairs - slots), (0, 0), (0, 0)))
    spots = jnp.transpose(every_block, (1, 0, 2)).reshape(targets, 1, 1, -1).astype(BF16)
    spots = jnp.pad(spots, ((0, 0), (0, pairs - 1), (0, 1), (0, LANES - spots.shape[3])))
    aux = jnp.concatenate([triple.reshape(targets, pairs, 6, width), spots], axis=2)
    return jnp.concatenate(
        [
            jnp.transpose(values, (1, 0, 2, 3)).reshape(targets, slots * channels, width),
            aux.reshape(targets, pairs * 8, width),
        ],
        axis=1,
    )


BLOCKS = 16
PARTS = 4
GROUP = 4
UNITS = 4


def group_limit(tiles):
    return (tiles + BLOCKS * (GROUP - 1)) // GROUP


def plan_kernel(slots, early, spot_row, got_ref, out_ref):
    senders = got_ref.shape[0]
    tiles = 2 * senders
    spots = jnp.transpose(got_ref[:, spot_row, :].astype(F32))
    kind = lax.broadcasted_iota(jnp.int32, (BLOCKS, tiles), 0).astype(F32)
    hits = []
    for slot in range(slots):
        row = jnp.concatenate([spots[2 * slot : 2 * slot + 1], spots[2 * slot + 1 : 2 * slot + 2]], axis=1)
        hits.append(jnp.where(kind == row, 1.0, 0.0))
    hit = jnp.concatenate(hits, axis=0)
    earlier = lax.broadcasted_iota(jnp.int32, (tiles, tiles), 0) < lax.broadcasted_iota(jnp.int32, (tiles, tiles), 1)
    rank = jnp.dot(hit.astype(BF16), jnp.where(earlier, 1.0, 0.0).astype(BF16), preferred_element_type=F32)
    count = jnp.sum(hit, axis=1, keepdims=True)
    groups = jnp.broadcast_to(jnp.floor((count + (GROUP - 1)) * (1.0 / GROUP)), (slots * BLOCKS, LANES))
    above = lax.broadcasted_iota(jnp.int32, (slots * BLOCKS,) * 2, 0)
    across = lax.broadcasted_iota(jnp.int32, (slots * BLOCKS,) * 2, 1)
    lower = jnp.where((above > across) & ((above >> 4) == (across >> 4)), 1.0, 0.0).astype(BF16)
    begin = jnp.dot(lower, groups.astype(BF16), preferred_element_type=F32)
    number = lax.broadcasted_iota(jnp.int32, (BLOCKS, LANES), 1).astype(F32)
    index = lax.broadcasted_iota(jnp.int32, (8, tiles), 1)
    kinds = jnp.where(lax.broadcasted_iota(jnp.int32, (8, tiles), 0) == 0, index, 1).astype(F32).astype(BF16)
    place = lax.broadcasted_iota(jnp.int32, (GROUP * LANES, tiles), 0).astype(F32)
    most = [jnp.zeros((1, LANES), F32)] * 2
    rows = []
    for slot in range(slots):
        part = slice(slot * BLOCKS, (slot + 1) * BLOCKS)
        start, size = begin[part], groups[part]
        wide = jnp.concatenate([start, start], axis=1)
        fours = jnp.floor(rank[part] * (1.0 / GROUP))
        spot = wide + fours + LANES * (rank[part] - GROUP * fours)
        spot = jnp.sum(hit[part] * spot, axis=0, keepdims=True)
        chosen = jnp.where(place == spot, 1.0, 0.0).astype(BF16)
        order = lax.dot_general(kinds, chosen, (((1,), (1,)), ((), ())), preferred_element_type=F32)
        taken = jnp.zeros((1, LANES), F32)
        for j in range(GROUP):
            tile = order[0:1, j * LANES : (j + 1) * LANES]
            second = jnp.where(tile >= LANES, 1.0, 0.0)
            turned = 1.0 - second if j & 1 else second
            rows.append(tile - LANES * second + LANES * turned)
            taken = taken + order[1:2, j * LANES : (j + 1) * LANES]
        block = jnp.sum(jnp.where(start + size <= number, 1.0, 0.0), axis=0, keepdims=True)
        rows.append(jnp.minimum(block, BLOCKS - 1.0) + BLOCKS * taken)
        which = 0 if slot < early else 1
        most[which] = jnp.maximum(most[which], start[BLOCKS - 1 :] + size[BLOCKS - 1 :])
    rows += [jnp.zeros((LANES - 2 - len(rows), LANES), F32)] + most
    table = jnp.transpose(jnp.concatenate(rows, axis=0))
    out_ref[...] = table[: out_ref.shape[0]].astype(jnp.int32)


def plan(got, slots_all, slots_here):
    senders = got.shape[0]
    spot_row = aux_row(slots_here, 0) + 6
    limit = -(-(group_limit(2 * senders) + 2 * UNITS) // 8) * 8
    return pl.pallas_call(
        functools.partial(plan_kernel, slots_all, slots_here, spot_row),
        in_specs=[pl.BlockSpec(memory_space=pltpu.VMEM)],
        out_specs=pl.BlockSpec(memory_space=pltpu.VMEM),
        out_shape=jax.ShapeDtypeStruct((limit, LANES), jnp.int32),
        name="plan",
    )(got)


def scatter_kernel(slots, offset, widths, plan_ref, got_ref, *rest):
    late = offset > 0
    extra_ref, out_ref, pack_ref, top_ref, bottom_ref, below_ref, held_ref = rest[:7]
    acc_refs = rest[7:]
    rows_out = out_ref.shape[1]

    lane = lax.broadcasted_iota(jnp.int32, (CH, LANES), 1)
    first = lane < LANES // 2
    first_aux = first[:8]
    sixteen = lax.broadcasted_iota(jnp.int32, (TILE, LANES), 0).astype(F32).astype(BF16)
    one_bf, zero_bf = jnp.ones((), BF16), jnp.zeros((), BF16)

    def gather(slot, number, held):
        values, auxes = [], []
        column = 5 * (offset + slot)
        info = plan_ref[number, column + 4]
        for j in range(GROUP):
            entry = plan_ref[number, column + j]
            sender = entry & (LANES - 1)
            turn = (entry & LANES) >> 1
            value = got_ref[sender, pl.ds(slot * CH, CH), :].astype(F32)
            aux = got_ref[sender, pl.ds(aux_row(slots, slot) // 8 * 8, 8), :].astype(F32)
            values.append(pltpu.roll(value, turn, 1))
            auxes.append(pltpu.roll(aux, turn, 1))
        live = (info >> 4) << 6
        for h in range(2):
            value = jnp.where(first, values[2 * h], values[2 * h + 1])
            held[h, :CH] = jnp.where(lane < live - h * LANES, value, 0.0)
            held[h, CH:] = jnp.where(first_aux, auxes[2 * h], auxes[2 * h + 1])

    def unit(slot, held):
        row = aux_row(slots, slot) % 8
        lefts, rights = [], []
        for h in range(2):
            value, aux = held[h, :CH], held[h, CH:]
            major = jnp.floor(aux * (1.0 / TILE))
            minor = aux - TILE * major
            by_x = value * aux[row + 1 : row + 2]
            frac_y = aux[row : row + 1]
            highs, lows = [value.astype(BF16)], []
            for part in (by_x, value * frac_y, by_x * frac_y):
                high = part.astype(BF16)
                highs.append(high)
                lows.append((part - high.astype(F32)).astype(BF16))
            lefts.append(jnp.concatenate(highs + lows, axis=0))
            spot = row + 2
            small = jnp.broadcast_to(minor[spot : spot + 1], (TILE, LANES)).astype(BF16)
            large = jnp.broadcast_to(major[spot : spot + 1], (TILE, LANES)).astype(BF16)
            one_hot = jnp.where(sixteen == small, one_bf, zero_bf)
            rights.append(
                jnp.concatenate(
                    [jnp.where(large == jnp.asarray(k, BF16), one_hot, zero_bf) for k in range(TILE)], axis=0
                )
            )
        return lax.dot_general(
            jnp.concatenate(lefts, axis=1), jnp.concatenate(rights, axis=1), (((1,), (1,)), ((), ())),
            preferred_element_type=F32,
        )

    def add(slot, info, sums):
        block = info & (BLOCKS - 1)
        for part in range(4):
            rows = pl.ds(part * CH, CH)
            total = sums[part * CH : (part + 1) * CH]
            if part:
                total = total + sums[(part + 3) * CH : (part + 4) * CH]
            acc_refs[slot][block, rows] += total

    units = [(slot, k) for k in range(UNITS) for slot in range(slots)]

    def fetch(number):
        for place, (slot, k) in enumerate(units):
            gather(slot, UNITS * number + k, held_ref.at[place])

    def several(number, carry):
        for place, (slot, k) in enumerate(units):
            sums = unit(slot, held_ref.at[place])
            add(slot, plan_ref[UNITS * number + k, 5 * (offset + slot) + 4], sums)
        fetch(number + 1)
        return carry

    for acc_ref in acc_refs:
        acc_ref[...] = jnp.zeros_like(acc_ref)
    fetch(0)
    lax.fori_loop(0, (plan_ref[0, LANES - 1 if late else LANES - 2] + UNITS - 1) // UNITS, several, 0)

    lane_group = lane >> 4
    for slot in range(slots):
        acc_ref = acc_refs[slot]

        def part(number, carry, slot=slot, acc_ref=acc_ref):
            band = number >> 1
            half = number & 1
            straight = [jnp.zeros((CH, LANES), F32)] * 8
            under = [jnp.zeros((CH, LANES), F32)] * 8
            for column in range(8):
                tile = acc_ref[band * 8 + column, :, pl.ds(pl.multiple_of(half * LANES, LANES), LANES)]
                a_0, a_x = tile[:CH], tile[CH : 2 * CH]
                a_y, a_xy = tile[2 * CH : 3 * CH], tile[3 * CH :]
                x_only, y_only = a_x - a_xy, a_y - a_xy
                here = a_0 - a_x - y_only + pltpu.roll(x_only, 1, 1)
                next_row = y_only + pltpu.roll(a_xy, 1, 1)
                for y in range(8):
                    hit = lane_group == ((y + column) & 7)
                    straight[y] = jnp.where(hit, here, straight[y])
                    under[y] = jnp.where(hit, next_row, under[y])
            for y in range(8):
                turn = (-16 * y) % LANES
                row = band * 16 + half * 8 + y
                out_ref[slot, row] = pltpu.roll(straight[y], turn, 1) if turn else straight[y]
                below_ref[row] = pltpu.roll(under[y], turn, 1) if turn else under[y]
            return carry

        lax.fori_loop(0, 4, part, 0, unroll=PARTS)
        out_ref[slot, 1:] += below_ref[: rows_out - 1]

    starts, _ = offsets_of(widths)
    jobs = [(out_ref.at[k], starts[offset + k], widths[offset + k]) for k in range(min(slots, len(widths) - 1 - offset))]
    if not late:
        jobs.append((extra_ref, starts[-1], widths[-1]))
    spot = 0
    for source, _, width in jobs:
        top_ref[spot : spot + width] = source[:width]
        bottom_ref[spot : spot + width] = source[rows_out - width :]
        spot += width
    per_group = rows_out // GROUPS

    def pack(row, carry):
        total = extra_ref[row] if late else jnp.zeros((CH, LANES), F32)
        for group in range(GROUPS):
            for source, start, width in jobs:
                value = source[group * per_group + row]
                begin = group * SPAN + 2 * start
                hit = (lane >= begin) & (lane < begin + 2 * width)
                turn = (begin + width) % LANES
                total = jnp.where(hit, pltpu.roll(value, turn, 1) if turn else value, total)
        pack_ref[row] = total
        return carry

    lax.fori_loop(0, per_group, pack, 0, unroll=4)


ROWS = 8
GROUPS = 2
SPAN = LANES // GROUPS


def scatter(got, table, slots, offset, rows_out, widths, *extra):
    carried = sum(widths[offset:-1]) if offset else sum(widths[:slots]) + widths[-1]
    shapes = [(slots, rows_out, CH, LANES)]
    shapes += [(rows_out // GROUPS, CH, LANES)] + [(carried, CH, LANES)] * 2
    vmem = pl.BlockSpec(memory_space=pltpu.VMEM)
    return pl.pallas_call(
        functools.partial(scatter_kernel, slots, offset, widths),
        in_specs=[pl.BlockSpec(memory_space=pltpu.SMEM), vmem] + [vmem for e in extra],
        out_specs=[vmem for s in shapes],
        scratch_shapes=[
            pltpu.VMEM((rows_out, CH, LANES), F32),
            pltpu.VMEM((UNITS * slots, 2, CH + 8, LANES), F32),
        ]
        + [pltpu.VMEM((BLOCKS, 4 * CH, 2 * LANES), F32)] * slots,
        out_shape=[jax.ShapeDtypeStruct(s, F32) for s in shapes],
        name="scatter",
    )(table, got, *extra)


def march_kernel(
    widths, halo, early, edge_ref, first_ref, second_ref, wind_ref, above_a, above_b, below_a, below_b,
    ends_ref, mix_ref, out_ref, field_ref, extra_ref, mixed_ref, turn_ref,
):
    rows_own = first_ref.shape[1]
    tall = rows_own + 2 * halo
    per_group = ends_ref.shape[0]
    starts, _ = offsets_of(widths)
    lane = lax.broadcasted_iota(jnp.int32, (CH, LANES), 1)
    main = pl.ds(0, LANES)
    side = pl.ds(LANES, LANES)
    steps = len(widths) - 1
    sources = [first_ref.at[k] for k in range(early)]
    sources += [second_ref.at[k] for k in range(steps - early)] + [wind_ref]

    for slot, (start, width) in enumerate(zip(starts, widths)):
        lo, hi = halo - width, halo + rows_own + width
        extra_ref[slot, hi : hi + ROWS] = jnp.zeros((ROWS, CH, 2 * LANES), F32)
        from_a = slot < early or slot == steps
        spot = sum(widths[:early]) if slot == steps else start if from_a else start - sum(widths[:early]) + halo
        extra_ref[slot, lo:halo, :, main] = (above_a if from_a else above_b)[spot : spot + width]
        extra_ref[slot, halo : halo + rows_own, :, main] = sources[slot][...]
        extra_ref[slot, halo + rows_own : hi, :, main] = (below_a if from_a else below_b)[spot : spot + width]

    def edge(ends, group, start, width):
        turn = -(group * SPAN + 2 * start + width) % LANES
        kept = (lane < width) | (lane >= LANES - width)
        return jnp.where(kept, pltpu.roll(ends, turn, 1) if turn else ends, 0.0)

    def edges(row, carry):
        ends = ends_ref[row]
        for group in range(GROUPS):
            for slot, (start, width) in enumerate(zip(starts, widths)):
                extra_ref[slot, halo + group * per_group + row, :, side] = edge(ends, group, start, width)
        return carry

    lax.fori_loop(0, per_group, edges, 0, unroll=4)
    for slot, (start, width) in enumerate(zip(starts, widths)):
        for i in range(width):
            spot = halo - width + i
            extra_ref[slot, spot, :, side] = edge(above_b[spot], GROUPS - 1, start, width)
            extra_ref[slot, halo + rows_own + i, :, side] = edge(below_b[i], 0, start, width)

    extra_ref[0, tall:] = jnp.zeros((extra_ref.shape[1] - tall, CH, 2 * LANES), F32)
    field_ref[...] = jnp.zeros_like(field_ref)
    mixed_ref[tall:] = jnp.zeros((mixed_ref.shape[0] - tall, CH, 2 * LANES), F32)
    matrix = mix_ref[...]
    wind = extra_ref.at[steps]
    half = CH // 2

    def mix(source, begin, count):
        for number in range(count):
            rows = pl.ds(begin + 8 * number, 8)
            field = source[rows].reshape(8 * CH, 2 * LANES)
            high = field.astype(BF16)
            low = (field - high.astype(F32)).astype(BF16)
            product = lax.dot_general(
                matrix, jnp.concatenate([high, high, low], axis=0), (((1,), (0,)), ((), ())),
                preferred_element_type=F32,
            )
            mixed_ref[rows] = product.reshape(8, CH, 2 * LANES)

    def twice(value):
        return jnp.concatenate([value, value], axis=0)

    for number in range(steps):
        reach = widths[number]
        source = extra_ref.at[0] if number == 0 else field_ref.at[number % 2]
        target = field_ref.at[(number + 1) % 2]
        begin, end = halo - reach, halo + rows_own + reach
        last = number == steps - 1
        mix(source, begin, -(-(end - begin) // 8))

        def pair(index, carry, target=target, begin=begin, last=last, number=number):
            for offset in range(ROWS):
                row = begin + 1 + ROWS * index + offset
                mixed = mixed_ref[row]
                u_half = twice(wind[row, :half]) * 0.5
                result = (1.0 - 4.0 * KAPPA) * mixed
                result = result + pltpu.roll((KAPPA + u_half) * mixed, 2 * LANES - 1, 1)
                result = result + pltpu.roll((KAPPA - u_half) * mixed, 1, 1)
                result = result + (KAPPA + 0.5 * twice(wind[row + 1, half:])) * mixed_ref[row + 1]
                result = result + (KAPPA - 0.5 * twice(wind[row - 1, half:])) * mixed_ref[row - 1]
                if last:
                    turn_ref[row - halo] = result[:, :LANES] + second_ref[steps - early, row - halo]
                else:
                    target[row] = result + extra_ref[number + 1, row]
            return carry

        lax.fori_loop(0, -(-(end - begin - 2) // ROWS), pair, 0)
        if not last:

            @pl.when(edge_ref[0] == 1)
            def _(target=target):
                target[:halo] = jnp.zeros((halo, CH, 2 * LANES), F32)

            @pl.when(edge_ref[1] == 1)
            def _(target=target):
                target[halo + rows_own : tall] = jnp.zeros((halo, CH, 2 * LANES), F32)

    for channel in range(CH):
        out_ref[channel] = turn_ref[:, channel, :]


def march(edge, first, second, wind, above, below, ends, mix, widths, halo):
    rows_own = first.shape[1]
    tall = rows_own + 2 * halo
    vmem = pl.BlockSpec(memory_space=pltpu.VMEM)
    return pl.pallas_call(
        functools.partial(march_kernel, widths, halo, first.shape[0]),
        in_specs=[pl.BlockSpec(memory_space=pltpu.SMEM)] + [vmem] * 9,
        out_specs=vmem,
        out_shape=jax.ShapeDtypeStruct((CH, rows_own, LANES), F32),
        scratch_shapes=[
            pltpu.VMEM((2, tall + 8, CH, 2 * LANES), F32),
            pltpu.VMEM((len(widths), tall + 8, CH, 2 * LANES), F32),
            pltpu.VMEM((tall + 8, CH, 2 * LANES), F32),
            pltpu.VMEM((rows_own, CH, LANES), F32),
        ],
        name="march",
    )(edge, first, second, wind, *above, *below, ends, mix)


def west_lanes(widths):
    lane = lax.broadcasted_iota(jnp.int32, (1, 1, LANES), 2) % SPAN
    starts, _ = offsets_of(widths)
    found = lane < 0
    for start, width in zip(starts, widths):
        found = found | ((lane >= 2 * start) & (lane < 2 * start + width))
    return found


def mix_matrix(channel_mix):
    rounded = lax.reduce_precision(channel_mix.T, 8, 7)
    high = rounded.astype(BF16)
    low = (channel_mix.T - rounded).astype(BF16)
    eye = jnp.eye(8, dtype=BF16)
    return jnp.concatenate([jnp.kron(eye, high), jnp.kron(eye, low), jnp.kron(eye, high)], axis=1)


def ring(axis, wrap):
    count = lax.axis_size(axis)
    up = [(i, (i + 1) % count) for i in range(count if wrap else count - 1)]
    return up, [(j, i) for i, j in up]


def program(innovations, fractions, cell_index, counts, blocks, u_wind, v_wind, channel_mix):
    slots = innovations.shape[0]
    rows_own = u_wind.shape[1]
    halo = slots - 1
    widths = tuple(range(halo, 0, -1)) + (halo,)
    early = CHUNK_A
    got = []
    for name, low, high in (("move_a", slots - early, slots), ("move_b", 0, slots - early)):
        parts = [x[low:high][::-1] for x in (innovations, fractions, cell_index, counts, blocks)]
        payload = build_payload(*parts, blocks[::-1] if name == "move_a" else parts[4])
        got.append(lax.all_to_all(payload, AXES, split_axis=0, concat_axis=0, tiled=True))
    u_rows, v_rows = jnp.transpose(u_wind, (1, 0, 2)), jnp.transpose(v_wind, (1, 0, 2))
    wind = jnp.concatenate([u_rows, u_rows, v_rows, v_rows], axis=1)
    table = plan(got[0], slots, early)
    first, pack_a, top_a, bottom_a = scatter(got[0], table, early, 0, rows_own, widths, wind)
    up, down = ring("lat", False)
    above_a, below_a = lax.ppermute(bottom_a, "lat", up), lax.ppermute(top_a, "lat", down)
    second, pack, top_b, bottom_b = scatter(got[1], table, slots - early, early, rows_own, widths, pack_a)
    around, back = ring("lon", True)
    west = lax.ppermute(pack, "lon", around)
    east = lax.ppermute(pack, "lon", back)
    ends = jnp.where(west_lanes(widths), west, east)
    last_up = jnp.concatenate([ends[-halo:], bottom_b])
    last_down = jnp.concatenate([ends[:halo], top_b])
    above = [above_a, lax.ppermute(last_up, "lat", up)]
    below = [below_a, lax.ppermute(last_down, "lat", down)]
    lat_index = lax.axis_index("lat")
    edge = jnp.stack([lat_index == 0, lat_index == lax.axis_size("lat") - 1]).astype(jnp.int32)
    field = march(edge, first, second, wind, above, below, ends, mix_matrix(channel_mix), widths, halo)
    return field.reshape(VARS, LEV, rows_own, u_wind.shape[2])


def solution(mesh):
    in_specs = (
        P(None, ("lon", "lat"), None, None),
        P(None, ("lon", "lat"), None, None),
        P(None, ("lon", "lat"), None),
        P(None, ("lon", "lat"), None),
        P(None, ("lon", "lat"), None),
        P(None, "lat", "lon"),
        P(None, "lat", "lon"),
        P(),
    )
    out_specs = P(None, None, "lat", "lon")
    return jax.shard_map(program, mesh=mesh, in_specs=in_specs, out_specs=out_specs, check_vma=False)
```
